512 devices in a mesh: gossip: 16 (over z, y_lo), shard: 32 (over x, y_hi, core).
Axes of the slice: x: 4, y: 8 (y_hi: 4, y_lo: 2; y = y_hi * 2 + y_lo), z: 8, core: 2. Of those that a mesh axis runs over, the one named last changes fastest.
Arguments:
- inputs: bfloat16 [16, 13824, 2020], P('gossip', 'shard'), may hold values from -6 to 6
- upstream: bfloat16 [16, 13824, 1010], P('gossip', 'shard'), may hold values from -6 to 6
- params: float32 [16, 2048, 1010], P('gossip', 'shard'), may hold values from -0.125 to 0.125
- ps_weight: float32 [16], P('gossip'), may hold values from 0.5 to 2
- step: int32 [1], replicated, may hold values from 0 to 999
- cycle_order: int32 [16], replicated, may hold values from 0 to 15, each once
Outputs:
- grad_in: bfloat16 [16, 13824, 2020], P('gossip', 'shard')
- new_params: float32 [16, 2048, 1010], P('gossip', 'shard')
- new_weight: float32 [16], P('gossip')
The draws below stay inside these ranges and needn't reach their ends.
Inputs may be any that keep to these rules, and one draw needn't show every extreme that they name: cycle_order names every group once.
All inputs are finite; a program needn't handle non-finite values.
Results may differ from the reference program's by a relative error of at most 0.0061.
Values may be sent and summed in bfloat16 or wider, within the bound.
No kernel may reach another device: no remote copies, remote signals or barrier semaphores. Data moves between devices by JAX's collectives and lax.ppermute only.
A program may use at most 64 MiB of HBM per device.

```python
import math
import jax
import jax.numpy as jnp
from jax import lax

WIDTH = 2020
GROUP_WIDTH = 1010
ROWS_DEV = 432
TOKENS = 13824
WIDTH_PAD = 2048
N_GOSSIP = 16
N_SHARD = 32


def block_scale(key, extent, split, low, largest):
    factor_of = 1.0
    for axis_at, blocks in split:
        heights = jax.random.uniform(jax.random.fold_in(jax.random.fold_in(key, 6), axis_at), (blocks,), jnp.float32, low / len(split), largest / len(split))
        factor_of = factor_of * jnp.repeat(jnp.exp(heights), extent[axis_at] // blocks).reshape((-1,) + (1,) * (len(extent) - 1 - axis_at))
    return factor_of


def scatter_about(rng, extent, width, most, split=(), kind=jnp.bfloat16):
    entries = width * jax.random.normal(rng, extent, jnp.float32)
    if split:
        entries = entries * block_scale(rng, extent, split, -0.22, 0.18)
    return jnp.clip(entries, -most, most).astype(kind)


def setup_inputs(seed: int = 0) -> dict:
    key_of = jax.random.split(jax.random.key(seed), 7)
    inputs = scatter_about(key_of[0], (N_GOSSIP, TOKENS, WIDTH), 1.0, 6.0, ((0, 16), (1, 32)))
    upstream = scatter_about(key_of[1], (N_GOSSIP, TOKENS, GROUP_WIDTH), 1.0, 6.0, ((0, 16), (1, 32)))
    params = scatter_about(key_of[2], (N_GOSSIP, WIDTH_PAD, GROUP_WIDTH), WIDTH ** -0.5, 0.125, ((0, 16), (1, 32)), jnp.float32)
    ps_weight = jnp.clip(jnp.exp(math.log(2.0) - 1.3862944 * jax.random.uniform(key_of[3], (N_GOSSIP,), jnp.float32) ** block_scale(key_of[3], (N_GOSSIP,), ((0, 16),), -0.2, 0.2)), 0.5, 2.0)
    step = jax.random.randint(key_of[4], (1,), 0, 1000).astype(jnp.int32)
    cycle_order = jax.random.permutation(key_of[5], N_GOSSIP).astype(jnp.int32)
    return dict(inputs=inputs, upstream=upstream, params=params, ps_weight=ps_weight, step=step, cycle_order=cycle_order)


learn_rate = 0.5


def one_group(x_rows, up_rows, own_shard, weight):
    debiased = (own_shard / weight).astype(jnp.bfloat16)
    in_rows = debiased[:WIDTH]
    pre_act = jnp.dot(x_rows, in_rows, preferred_element_type=jnp.float32)
    sigmoid_pre = jax.nn.sigmoid(pre_act)
    d_pre = (up_rows.astype(jnp.float32) * sigmoid_pre * (1.0 + pre_act * (1.0 - sigmoid_pre))).astype(jnp.bfloat16)
    grad_in = jnp.dot(d_pre, in_rows.T, preferred_element_type=jnp.float32).astype(jnp.bfloat16)
    token_blocks = x_rows.reshape(N_SHARD, ROWS_DEV, WIDTH)
    grad_blocks = d_pre.reshape(N_SHARD, ROWS_DEV, GROUP_WIDTH)

    def add_block(running, paired):
        partial_value = jnp.dot(paired[0].T, paired[1], preferred_element_type=jnp.float32)
        partial_value = lax.optimization_barrier(partial_value.astype(jnp.bfloat16)).astype(jnp.float32)
        return running + partial_value, None

    summed, _ = lax.scan(add_block, jnp.zeros((WIDTH, GROUP_WIDTH), jnp.float32), (token_blocks, grad_blocks))
    summed = jnp.pad(summed, ((0, WIDTH_PAD - WIDTH), (0, 0)))
    stepped = own_shard - learn_rate * summed / TOKENS
    return grad_in, stepped


def reference(inputs, upstream, params, ps_weight, step, cycle_order):
    grad_in, stepped = lax.map(lambda packed: one_group(*packed), (inputs, upstream, params, ps_weight))
    levels = N_GOSSIP.bit_length() - 1
    distance = jnp.left_shift(jnp.int32(1), (step[0] % levels).astype(jnp.int32))
    ordinal = jnp.arange(N_GOSSIP, dtype=jnp.int32)
    matches = cycle_order[:, None] == ordinal[None, :]
    position = jnp.sum(jnp.where(matches, ordinal[:, None], 0), axis=0).astype(jnp.int32)
    source_pos = (position - distance) % N_GOSSIP
    sources = jnp.sum(jnp.where(source_pos[:, None] == ordinal[None, :], cycle_order[None, :], 0), axis=1).astype(jnp.int32)
    new_params = 0.5 * stepped + 0.5 * stepped[sources]
    new_weight = 0.5 * ps_weight + 0.5 * ps_weight[sources]
    return grad_in, new_params, new_weight
```

```python
import functools

import jax
import jax.numpy as jnp
from jax import lax
from jax.experimental import pallas as pl
from jax.experimental.pallas import tpu as pltpu
from jax.sharding import PartitionSpec as P

LEARN_RATE = 0.5
NX, NY = 4, 4
ROWS = 64
LANES = 1024


def mask_of(core, j):
    return (0, 1 + 2 * core, 3 - 2 * core, 2)[j]


def place(sid):
    return sid // 8, (sid // 2) % 4, sid % 2


def pairs(axis, stage):
    out = []
    for s in range(2 * NX * NY):
        x, y, c = s // 8, (s // 2) % 4, s % 2
        if axis == "core":
            c ^= 1
        elif axis == "x":
            x ^= mask_of(c, stage)
        else:
            y ^= mask_of(c, stage)
        out.append((s, (x * NY + y) * 2 + c))
    return out


def send(v, axis, stage=0):
    return lax.ppermute(v, "shard", pairs(axis, stage))


def vmem():
    return pl.BlockSpec(memory_space=pltpu.VMEM)


def smem():
    return pl.BlockSpec(memory_space=pltpu.SMEM)


def params(mib):
    return pltpu.CompilerParams(vmem_limit_bytes=mib << 20)


def tile_at(sid, k, i, partner):
    x, y, core = place(sid)
    core = jnp.where(partner, 1 - core, core)
    first, second = 1 + 2 * core, 3 - 2 * core
    jx, q = k // 2, k % 2
    mx = jnp.where(jx == 0, 0, jnp.where(jx == 1, first, jnp.where(jx == 2, second, 2)))
    my = jnp.where(q == 0, first * i, jnp.where(i == 0, second, 2))
    return (x ^ mx) * NY + (y ^ my)


def split_kernel(width, sid_ref, k0, k1, s0, s1, keep_ref, send_ref):
    k = pl.program_id(0)
    core = sid_ref[0] % 2
    for partner, refs, out_ref in ((False, (k0, k1), keep_ref), (True, (s0, s1), send_ref)):
        tiles = []
        for i, ref in enumerate(refs):
            t = ref[...].astype(jnp.float32)
            col = tile_at(sid_ref[0], k, i, partner) * 128 + lax.broadcasted_iota(jnp.int32, t.shape, 1)
            tiles.append(jnp.where(col < width, t, 0.0))
        t0, t1 = tiles
        r0, r1 = pltpu.roll(t0, 64, 1), pltpu.roll(t1, 64, 1)
        low = lax.broadcasted_iota(jnp.int32, t0.shape, 1) < 64
        even = jnp.where(low, t0, r1)
        odd = jnp.where(low, r0, t1)
        parity = 1 - core if partner else core
        out_ref[...] = jnp.where(parity == 0, even, odd).astype(jnp.bfloat16)


def split_by_core(sid, x):
    rows, width = x.shape

    def spec(i, partner):
        return pl.BlockSpec((rows, 128), lambda k, sid_ref: (0, tile_at(sid_ref[0], k, i, partner)))

    half = jax.ShapeDtypeStruct((rows, NX * NY * ROWS), jnp.bfloat16)
    return pl.pallas_call(
        functools.partial(split_kernel, width),
        grid_spec=pltpu.PrefetchScalarGridSpec(
            num_scalar_prefetch=1,
            grid=(8,),
            in_specs=[spec(0, False), spec(1, False), spec(0, True), spec(1, True)],
            out_specs=[pl.BlockSpec((rows, 128), lambda k, sid_ref: (0, k))] * 2,
        ),
        out_shape=[half, half],
        compiler_params=params(8),
        cost_estimate=pl.CostEstimate(flops=rows * 2048 * 4, bytes_accessed=rows * 8192, transcendentals=0),
        name="split_by_core",
    )(sid, x, x, x, x)


def forward_kernel(xk_ref, xs_ref, up_ref, a0, a1, b0, b1, d_ref):
    cols = up_ref.shape[1]
    z = None
    for x_ref, refs in ((xk_ref, (a0, a1)), (xs_ref, (b0, b1))):
        for i, ref in enumerate(refs):
            term = jnp.dot(x_ref[:, 512 * i:512 * i + 512], ref[...], preferred_element_type=jnp.float32)
            z = term if z is None else z + term
    z = z[:, :cols]
    s = 1.0 / (1.0 + jnp.exp(-z))
    d = up_ref[...].astype(jnp.float32) * s * (1.0 + z * (1.0 - s))
    d_ref[:, 896:] = jnp.zeros((d_ref.shape[0], 128), jnp.bfloat16)
    d_ref[:, :cols] = d.astype(jnp.bfloat16)


def forward(xk, xs, up, a0, a1, b0, b1):
    rows, cols = up.shape
    half = NX * NY * ROWS
    return pl.pallas_call(
        forward_kernel,
        in_specs=[vmem()] * 7,
        out_specs=vmem(),
        out_shape=jax.ShapeDtypeStruct((rows, LANES), jnp.bfloat16),
        compiler_params=params(28),
        cost_estimate=pl.CostEstimate(flops=4 * rows * half * cols, bytes_accessed=8 << 20, transcendentals=rows * cols),
        name="forward",
    )(xk, xs, up, a0, a1, b0, b1)


def back_kernel(width, sid_ref, d_ref, a0, a1, b0, b1, out_ref, wv, sem):
    cx, cy, core = place(sid_ref[0])
    for k, src in enumerate((a0, a1, b0, b1)):
        c = core if k < 2 else 1 - core
        for jx in range(2):
            for jy in range(4):
                bx = cx ^ mask_of(c, jx + 2 * (k % 2))
                by = cy ^ mask_of(c, jy)
                row = pl.multiple_of(((bx * NY + by) * 2 + c) * ROWS, ROWS)
                pltpu.make_async_copy(
                    src.at[pl.ds((jx * 4 + jy) * ROWS, ROWS)], wv.at[pl.ds(row, ROWS)], sem
                ).start()
    pltpu.make_async_copy(wv, wv, sem).wait()
    dims = (((1,), (1,)), ((), ()))
    for n in range(4):
        g = lax.dot_general(d_ref[...], wv[512 * n:512 * n + 512], dims, preferred_element_type=jnp.float32)
        take = min(512, width - 512 * n)
        out_ref[:, 512 * n:512 * n + take] = g[:, :take].astype(jnp.bfloat16)


def back(sid, width, d, a0, a1, b0, b1):
    rows, cols = d.shape
    return pl.pallas_call(
        functools.partial(back_kernel, width),
        in_specs=[smem(), vmem()] + [pl.BlockSpec(memory_space=pl.ANY)] * 4,
        out_specs=vmem(),
        out_shape=jax.ShapeDtypeStruct((rows, width), jnp.bfloat16),
        scratch_shapes=[pltpu.VMEM((2048, LANES), jnp.bfloat16), pltpu.SemaphoreType.DMA],
        compiler_params=params(20),
        cost_estimate=pl.CostEstimate(flops=2 * rows * 2048 * cols, bytes_accessed=8 << 20, transcendentals=0),
        name="back",
    )(sid, d, a0, a1, b0, b1)


def partial_kernel(first, xk_ref, xr_ref, d_ref, dr_ref, out_ref):
    dims = (((0,), (0,)), ((), ()))
    at = slice(256 * first, 256 * first + 512)
    r = lax.dot_general(xk_ref[:, at], d_ref[...], dims, preferred_element_type=jnp.float32)
    r = r + lax.dot_general(xr_ref[:, at], dr_ref[...], dims, preferred_element_type=jnp.float32)
    out_ref[...] = r.astype(jnp.bfloat16)


def partial(first, xk, xr, d, dr):
    rows, cols = d.shape
    return pl.pallas_call(
        functools.partial(partial_kernel, first),
        in_specs=[vmem()] * 4,
        out_specs=vmem(),
        out_shape=jax.ShapeDtypeStruct((512, cols), jnp.bfloat16),
        compiler_params=params(20),
        cost_estimate=pl.CostEstimate(flops=4 * rows * 512 * cols, bytes_accessed=4 << 20, transcendentals=0),
        name="partial_%d" % first,
    )(xk, xr, d, dr)


def pack_kernel(scale, sid_ref, w_ref, p_ref, keep_ref, got_ref, own_ref, pack_ref):
    _, cy, core = place(sid_ref[0])
    rows, cols = p_ref.shape
    tail = cols - 7 * 128
    w = jnp.full((32, 128), w_ref[0], jnp.float32)
    hi = w.astype(jnp.bfloat16).astype(jnp.float32)
    lane = lax.broadcasted_iota(jnp.int32, (32, 128), 1)
    spare = jnp.where(lane == 126, hi, jnp.where(lane == 127, w - hi, 0.0)).astype(jnp.bfloat16)
    for jy in range(NY):
        at = slice(ROWS * jy, ROWS * jy + ROWS)
        v = scale * (keep_ref[at].astype(jnp.float32) + got_ref[at].astype(jnp.float32))
        if jy == 0:
            own = p_ref[...] + v[:, :cols]
            own_ref[...] = own
        y = cy ^ mask_of(core, jy)
        for h in range(2):
            for j in range(8):
                to = y * 16 + 8 * h + j
                if jy == 0 and j == 7:
                    pack_ref[to] = spare
                    pack_ref[to, :, :tail] = own[32 * h:32 * h + 32, 896:].astype(jnp.bfloat16)
                elif jy == 0:
                    pack_ref[to] = own[32 * h:32 * h + 32, 128 * j:128 * j + 128].astype(jnp.bfloat16)
                else:
                    pack_ref[to] = v[32 * h:32 * h + 32, 128 * j:128 * j + 128].astype(jnp.bfloat16)


def pack(scale, sid, weight, own, keep, got):
    return pl.pallas_call(
        functools.partial(pack_kernel, scale),
        in_specs=[smem(), smem()] + [vmem()] * 3,
        out_specs=[vmem(), vmem()],
        out_shape=[
            jax.ShapeDtypeStruct(own.shape, jnp.float32),
            jax.ShapeDtypeStruct((64, 32, 128), jnp.bfloat16),
        ],
        compiler_params=params(8),
        cost_estimate=pl.CostEstimate(flops=1 << 20, bytes_accessed=2 << 20, transcendentals=0),
        name="pack",
    )(sid, weight, own, keep, got)


def mix_kernel(sid_ref, gid_ref, step_ref, order_ref, in_ref, out_ref, total):
    _, cy, _ = place(sid_ref[0])
    for g in range(16):
        t = in_ref[g].astype(jnp.float32)
        for y in range(1, NY):
            t = t + in_ref[16 * y + g].astype(jnp.float32)
        total[g] = t
    lane = lax.broadcasted_iota(jnp.int32, (32, 128), 1)
    spare = (lane >= 126) & (gid_ref[0] % 8 == 7)
    distance = 1 << lax.rem(step_ref[0], 4)
    for p in range(16):
        m = order_ref[p]
        source = total[order_ref[(p - distance + 16) % 16]]
        rest = total[m] - in_ref[16 * cy + m].astype(jnp.float32)
        out_ref[m] = jnp.where(spare, source, 0.5 * (source + rest)).astype(jnp.bfloat16)


def mix(sid, gid, step, order, got):
    return pl.pallas_call(
        mix_kernel,
        in_specs=[smem()] * 4 + [vmem()],
        out_specs=vmem(),
        out_shape=jax.ShapeDtypeStruct((16, 32, 128), jnp.bfloat16),
        scratch_shapes=[pltpu.VMEM((16, 32, 128), jnp.float32)],
        compiler_params=params(8),
        cost_estimate=pl.CostEstimate(flops=1 << 20, bytes_accessed=1 << 20, transcendentals=0),
        name="mix",
    )(sid, gid, step, order, got)


def finish_kernel(w_ref, own_ref, got_ref, new_ref, new_w_ref):
    rows, cols = own_ref.shape
    for h in range(2):
        for j in range(8):
            width = min(128, cols - 128 * j)
            at = (slice(32 * h, 32 * h + 32), slice(128 * j, 128 * j + width))
            new_ref[at] = 0.5 * own_ref[at] + got_ref[8 * h + j].astype(jnp.float32)[:, :width]
    last = got_ref[7].astype(jnp.float32)
    lane = lax.broadcasted_iota(jnp.int32, last.shape, 1)
    row = lax.broadcasted_iota(jnp.int32, last.shape, 0)
    source_w = jnp.sum(jnp.where((lane >= 126) & (row == 0), last, 0.0))
    new_w_ref[0] = 0.5 * w_ref[0] + 0.5 * source_w


def finish(weight, own, got):
    return pl.pallas_call(
        finish_kernel,
        in_specs=[smem(), vmem(), vmem()],
        out_specs=[vmem(), smem()],
        out_shape=[
            jax.ShapeDtypeStruct(own.shape, jnp.float32),
            jax.ShapeDtypeStruct((1,), jnp.float32),
        ],
        compiler_params=params(8),
        name="finish",
    )(weight, own, got)


def add(a, b):
    return (a.astype(jnp.float32) + b.astype(jnp.float32)).astype(jnp.bfloat16)


def halves(a):
    n = a.shape[0] // 2
    return a[:n], a[n:]


def body(inputs, upstream, params, ps_weight, step, cycle_order):
    x_rows = inputs[0]
    up_rows = upstream[0]
    own_shard = params[0]
    n_shard = lax.axis_size("shard")
    n_groups = lax.axis_size("gossip")
    in_width = x_rows.shape[1]
    sid = lax.axis_index("shard").astype(jnp.int32).reshape(1)

    debiased = (own_shard / ps_weight[0]).astype(jnp.bfloat16)
    debiased = jnp.pad(debiased, ((0, 0), (0, LANES - debiased.shape[1])))
    x_keep, x_send = split_by_core(sid, x_rows)
    held = jnp.concatenate([debiased, send(debiased, "y", 1)])
    held = jnp.concatenate([held, send(held, "y", 2)])
    held = jnp.concatenate([held, send(held, "x", 1)])
    far = send(held, "x", 2)
    other_held = send(held, "core")
    far, x_keep, x_send = lax.optimization_barrier((far, x_keep, x_send))
    other_far = send(far, "core")
    x_got = send(x_send, "core")

    d_pre = forward(x_keep, x_send, up_rows, held, far, other_held, other_far)
    d_got = send(d_pre, "core")
    out = partial(2, x_keep, x_got, d_pre, d_got)
    got = send(out, "x", 2)
    keep = partial(0, x_keep, x_got, d_pre, d_got)
    grad_in = back(sid, in_width, d_pre, held, far, other_held, other_far)
    (k0, k1), (g0, g1) = halves(keep), halves(got)
    keep, out = add(k0, g0), add(k1, g1)
    got = send(out, "x", 1)

    tokens = x_rows.shape[0] * n_shard
    gid = lax.axis_index("gossip").astype(jnp.int32).reshape(1)
    own, pieces = pack(-LEARN_RATE / tokens, sid, ps_weight, own_shard, keep, got)
    planes = [
        [g * n_shard + (x * NY + y) * 2 + c for y in range(NY) for g in range(n_groups)]
        for x in range(NX) for c in range(2)
    ]
    received = lax.all_to_all(
        pieces, ("gossip", "shard"), split_axis=0, concat_axis=0, axis_index_groups=planes, tiled=True
    )
    outgoing = mix(sid, gid, step, cycle_order, received)
    arrived = lax.all_to_all(outgoing, "gossip", split_axis=0, concat_axis=0, tiled=True)
    new_params, new_weight = finish(ps_weight, own, arrived)
    return (grad_in[None], new_params[None], new_weight)


def solution(mesh):
    placed = (
        P("gossip", "shard", None),
        P("gossip", "shard", None),
        P("gossip", "shard", None),
        P("gossip"),
        P(),
        P(),
    )
    return jax.shard_map(
        body,
        mesh=mesh,
        in_specs=placed,
        out_specs=(P("gossip", "shard", None), P("gossip", "shard", None), P("gossip")),
        check_vma=False,
    )
```

```python
import functools

import jax
import jax.numpy as jnp
from jax import lax
from jax.experimental import pallas as pl
from jax.experimental.pallas import tpu as pltpu
from jax.sharding import PartitionSpec as P

LEARN_RATE = 0.5
NX, NY = 4, 4
ROWS = 64
LANES = 1024


def mask_of(core, j):
    return (0, 1 + 2 * core, 3 - 2 * core, 2)[j]


def place(sid):
    return sid // 8, (sid // 2) % 4, sid % 2


def pairs(axis, stage):
    out = []
    for s in range(2 * NX * NY):
        x, y, c = s // 8, (s // 2) % 4, s % 2
        if axis == "core":
            c ^= 1
        elif axis == "x":
            x ^= mask_of(c, stage)
        else:
            y ^= mask_of(c, stage)
        out.append((s, (x * NY + y) * 2 + c))
    return out


def send(v, axis, stage=0):
    return lax.ppermute(v, "shard", pairs(axis, stage))


def vmem():
    return pl.BlockSpec(memory_space=pltpu.VMEM)


def smem():
    return pl.BlockSpec(memory_space=pltpu.SMEM)


def params(mib):
    return pltpu.CompilerParams(vmem_limit_bytes=mib << 20)


def tile_at(sid, k, i, partner):
    x, y, core = place(sid)
    core = jnp.where(partner, 1 - core, core)
    first, second = 1 + 2 * core, 3 - 2 * core
    jx, q = k // 2, k % 2
    mx = jnp.where(jx == 0, 0, jnp.where(jx == 1, first, jnp.where(jx == 2, second, 2)))
    my = jnp.where(q == 0, first * i, jnp.where(i == 0, second, 2))
    return (x ^ mx) * NY + (y ^ my)


def split_kernel(width, sid_ref, k0, k1, s0, s1, keep_ref, send_ref):
    k = pl.program_id(0)
    core = sid_ref[0] % 2
    for partner, refs, out_ref in ((False, (k0, k1), keep_ref), (True, (s0, s1), send_ref)):
        tiles = []
        for i, ref in enumerate(refs):
            t = ref[...].astype(jnp.float32)
            col = tile_at(sid_ref[0], k, i, partner) * 128 + lax.broadcasted_iota(jnp.int32, t.shape, 1)
            tiles.append(jnp.where(col < width, t, 0.0))
        t0, t1 = tiles
        r0, r1 = pltpu.roll(t0, 64, 1), pltpu.roll(t1, 64, 1)
        low = lax.broadcasted_iota(jnp.int32, t0.shape, 1) < 64
        even = jnp.where(low, t0, r1)
        odd = jnp.where(low, r0, t1)
        parity = 1 - core if partner else core
        out_ref[...] = jnp.where(parity == 0, even, odd).astype(jnp.bfloat16)


def split_by_core(sid, x):
    rows, width = x.shape

    def spec(i, partner):
        return pl.BlockSpec((rows, 128), lambda k, sid_ref: (0, tile_at(sid_ref[0], k, i, partner)))

    half = jax.ShapeDtypeStruct((rows, NX * NY * ROWS), jnp.bfloat16)
    return pl.pallas_call(
        functools.partial(split_kernel, width),
        grid_spec=pltpu.PrefetchScalarGridSpec(
            num_scalar_prefetch=1,
            grid=(8,),
            in_specs=[spec(0, False), spec(1, False), spec(0, True), spec(1, True)],
            out_specs=[pl.BlockSpec((rows, 128), lambda k, sid_ref: (0, k))] * 2,
        ),
        out_shape=[half, half],
        compiler_params=params(8),
        cost_estimate=pl.CostEstimate(flops=rows * 2048 * 4, bytes_accessed=rows * 8192, transcendentals=0),
        name="split_by_core",
    )(sid, x, x, x, x)


def forward_kernel(xk_ref, xs_ref, up_ref, a0, a1, b0, b1, d_ref):
    cols = up_ref.shape[1]
    z = None
    for x_ref, refs in ((xk_ref, (a0, a1)), (xs_ref, (b0, b1))):
        for i, ref in enumerate(refs):
            term = jnp.dot(x_ref[:, 512 * i:512 * i + 512], ref[...], preferred_element_type=jnp.float32)
            z = term if z is None else z + term
    z = z[:, :cols]
    s = 1.0 / (1.0 + jnp.exp(-z))
    d = up_ref[...].astype(jnp.float32) * s * (1.0 + z * (1.0 - s))
    d_ref[:, 896:] = jnp.zeros((d_ref.shape[0], 128), jnp.bfloat16)
    d_ref[:, :cols] = d.astype(jnp.bfloat16)


def forward(xk, xs, up, a0, a1, b0, b1):
    rows, cols = up.shape
    half = NX * NY * ROWS
    return pl.pallas_call(
        forward_kernel,
        in_specs=[vmem()] * 7,
        out_specs=vmem(),
        out_shape=jax.ShapeDtypeStruct((rows, LANES), jnp.bfloat16),
        compiler_params=params(28),
        cost_estimate=pl.CostEstimate(flops=4 * rows * half * cols, bytes_accessed=8 << 20, transcendentals=rows * cols),
        name="forward",
    )(xk, xs, up, a0, a1, b0, b1)


def back_kernel(width, sid_ref, d_ref, a0, a1, b0, b1, out_ref, wv, sem):
    cx, cy, core = place(sid_ref[0])
    for k, src in enumerate((a0, a1, b0, b1)):
        c = core if k < 2 else 1 - core
        for jx in range(2):
            for jy in range(4):
                bx = cx ^ mask_of(c, jx + 2 * (k % 2))
                by = cy ^ mask_of(c, jy)
                row = pl.multiple_of(((bx * NY + by) * 2 + c) * ROWS, ROWS)
                pltpu.make_async_copy(
                    src.at[pl.ds((jx * 4 + jy) * ROWS, ROWS)], wv.at[pl.ds(row, ROWS)], sem.at[bx]
                ).start()
    dims = (((1,), (1,)), ((), ()))
    for n in range(4):
        at = pl.ds(512 * n, 512)
        pltpu.make_async_copy(wv.at[at], wv.at[at], sem.at[n]).wait()
        g = lax.dot_general(d_ref[...], wv[at], dims, preferred_element_type=jnp.float32)
        take = min(512, width - 512 * n)
        out_ref[:, 512 * n:512 * n + take] = g[:, :take].astype(jnp.bfloat16)


def back(sid, width, d, a0, a1, b0, b1):
    rows, cols = d.shape
    return pl.pallas_call(
        functools.partial(back_kernel, width),
        in_specs=[smem()] + [vmem()] * 5,
        out_specs=vmem(),
        out_shape=jax.ShapeDtypeStruct((rows, width), jnp.bfloat16),
        scratch_shapes=[pltpu.VMEM((2048, LANES), jnp.bfloat16), pltpu.SemaphoreType.DMA((4,))],
        compiler_params=params(20),
        cost_estimate=pl.CostEstimate(flops=2 * rows * 2048 * cols, bytes_accessed=8 << 20, transcendentals=0),
        name="back",
    )(sid, d, a0, a1, b0, b1)


def partial_kernel(first, xk_ref, xr_ref, d_ref, dr_ref, out_ref):
    dims = (((0,), (0,)), ((), ()))
    at = slice(256 * first, 256 * first + 512)
    r = lax.dot_general(xk_ref[:, at], d_ref[...], dims, preferred_element_type=jnp.float32)
    r = r + lax.dot_general(xr_ref[:, at], dr_ref[...], dims, preferred_element_type=jnp.float32)
    out_ref[...] = r.astype(jnp.bfloat16)


def partial(first, xk, xr, d, dr):
    rows, cols = d.shape
    return pl.pallas_call(
        functools.partial(partial_kernel, first),
        in_specs=[vmem()] * 4,
        out_specs=vmem(),
        out_shape=jax.ShapeDtypeStruct((512, cols), jnp.bfloat16),
        compiler_params=params(20),
        cost_estimate=pl.CostEstimate(flops=4 * rows * 512 * cols, bytes_accessed=4 << 20, transcendentals=0),
        name="partial_%d" % first,
    )(xk, xr, d, dr)


def pack_kernel(scale, sid_ref, w_ref, p_ref, keep_ref, got_ref, own_ref, pack_ref):
    _, cy, core = place(sid_ref[0])
    rows, cols = p_ref.shape
    tail = cols - 7 * 128
    w = jnp.full((32, 128), w_ref[0], jnp.float32)
    hi = w.astype(jnp.bfloat16).astype(jnp.float32)
    lane = lax.broadcasted_iota(jnp.int32, (32, 128), 1)
    spare = jnp.where(lane == 126, hi, jnp.where(lane == 127, w - hi, 0.0)).astype(jnp.bfloat16)
    for jy in range(NY):
        at = slice(ROWS * jy, ROWS * jy + ROWS)
        v = scale * (keep_ref[at].astype(jnp.float32) + got_ref[at].astype(jnp.float32))
        if jy == 0:
            own = p_ref[...] + v[:, :cols]
            own_ref[...] = own
        y = cy ^ mask_of(core, jy)
        for h in range(2):
            for j in range(8):
                to = y * 16 + 8 * h + j
                if jy == 0 and j == 7:
                    pack_ref[to] = spare
                    pack_ref[to, :, :tail] = own[32 * h:32 * h + 32, 896:].astype(jnp.bfloat16)
                elif jy == 0:
                    pack_ref[to] = own[32 * h:32 * h + 32, 128 * j:128 * j + 128].astype(jnp.bfloat16)
                else:
                    pack_ref[to] = v[32 * h:32 * h + 32, 128 * j:128 * j + 128].astype(jnp.bfloat16)


def pack(scale, sid, weight, own, keep, got):
    return pl.pallas_call(
        functools.partial(pack_kernel, scale),
        in_specs=[smem(), smem()] + [vmem()] * 3,
        out_specs=[vmem(), vmem()],
        out_shape=[
            jax.ShapeDtypeStruct(own.shape, jnp.float32),
            jax.ShapeDtypeStruct((64, 32, 128), jnp.bfloat16),
        ],
        compiler_params=params(8),
        cost_estimate=pl.CostEstimate(flops=1 << 20, bytes_accessed=2 << 20, transcendentals=0),
        name="pack",
    )(sid, weight, own, keep, got)


def mix_kernel(sid_ref, gid_ref, step_ref, order_ref, in_ref, out_ref, total):
    _, cy, _ = place(sid_ref[0])
    for g in range(16):
        t = in_ref[g].astype(jnp.float32)
        for y in range(1, NY):
            t = t + in_ref[16 * y + g].astype(jnp.float32)
        total[g] = t
    lane = lax.broadcasted_iota(jnp.int32, (32, 128), 1)
    spare = (lane >= 126) & (gid_ref[0] % 8 == 7)
    distance = 1 << lax.rem(step_ref[0], 4)
    for p in range(16):
        m = order_ref[p]
        source = total[order_ref[(p - distance + 16) % 16]]
        rest = total[m] - in_ref[16 * cy + m].astype(jnp.float32)
        out_ref[m] = jnp.where(spare, source, 0.5 * (source + rest)).astype(jnp.bfloat16)


def mix(sid, gid, step, order, got):
    return pl.pallas_call(
        mix_kernel,
        in_specs=[smem()] * 4 + [vmem()],
        out_specs=vmem(),
        out_shape=jax.ShapeDtypeStruct((16, 32, 128), jnp.bfloat16),
        scratch_shapes=[pltpu.VMEM((16, 32, 128), jnp.float32)],
        compiler_params=params(8),
        cost_estimate=pl.CostEstimate(flops=1 << 20, bytes_accessed=1 << 20, transcendentals=0),
        name="mix",
    )(sid, gid, step, order, got)


def finish_kernel(w_ref, own_ref, got_ref, new_ref, new_w_ref):
    rows, cols = own_ref.shape
    for h in range(2):
        for j in range(8):
            width = min(128, cols - 128 * j)
            at = (slice(32 * h, 32 * h + 32), slice(128 * j, 128 * j + width))
            new_ref[at] = 0.5 * own_ref[at] + got_ref[8 * h + j].astype(jnp.float32)[:, :width]
    last = got_ref[7].astype(jnp.float32)
    lane = lax.broadcasted_iota(jnp.int32, last.shape, 1)
    row = lax.broadcasted_iota(jnp.int32, last.shape, 0)
    source_w = jnp.sum(jnp.where((lane >= 126) & (row == 0), last, 0.0))
    new_w_ref[0] = 0.5 * w_ref[0] + 0.5 * source_w


def finish(weight, own, got):
    return pl.pallas_call(
        finish_kernel,
        in_specs=[smem(), vmem(), vmem()],
        out_specs=[vmem(), smem()],
        out_shape=[
            jax.ShapeDtypeStruct(own.shape, jnp.float32),
            jax.ShapeDtypeStruct((1,), jnp.float32),
        ],
        compiler_params=params(8),
        name="finish",
    )(weight, own, got)


def add(a, b):
    return (a.astype(jnp.float32) + b.astype(jnp.float32)).astype(jnp.bfloat16)


def halves(a):
    n = a.shape[0] // 2
    return a[:n], a[n:]


def body(inputs, upstream, params, ps_weight, step, cycle_order):
    x_rows = inputs[0]
    up_rows = upstream[0]
    own_shard = params[0]
    n_shard = lax.axis_size("shard")
    n_groups = lax.axis_size("gossip")
    in_width = x_rows.shape[1]
    sid = lax.axis_index("shard").astype(jnp.int32).reshape(1)

    debiased = (own_shard / ps_weight[0]).astype(jnp.bfloat16)
    debiased = jnp.pad(debiased, ((0, 0), (0, LANES - debiased.shape[1])))
    x_keep, x_send = split_by_core(sid, x_rows)
    held = jnp.concatenate([debiased, send(debiased, "y", 1)])
    held = jnp.concatenate([held, send(held, "y", 2)])
    held = jnp.concatenate([held, send(held, "x", 1)])
    far = send(held, "x", 2)
    other_held = send(held, "core")
    x_got = send(x_send, "core")
    far, x_keep, x_send, x_got = lax.optimization_barrier((far, x_keep, x_send, x_got))
    other_far = send(far, "core")

    d_pre = forward(x_keep, x_send, up_rows, held, far, other_held, other_far)
    d_got = send(d_pre, "core")
    out = partial(2, x_keep, x_got, d_pre, d_got)
    got = send(out, "x", 2)
    keep = partial(0, x_keep, x_got, d_pre, d_got)
    grad_in = back(sid, in_width, d_pre, held, far, other_held, other_far)
    got, grad_in = lax.optimization_barrier((got, grad_in))
    (k0, k1), (g0, g1) = halves(keep), halves(got)
    keep, out = add(k0, g0), add(k1, g1)
    got = send(out, "x", 1)

    tokens = x_rows.shape[0] * n_shard
    gid = lax.axis_index("gossip").astype(jnp.int32).reshape(1)
    own, pieces = pack(-LEARN_RATE / tokens, sid, ps_weight, own_shard, keep, got)
    planes = [
        [g * n_shard + (x * NY + y) * 2 + c for y in range(NY) for g in range(n_groups)]
        for x in range(NX) for c in range(2)
    ]
    received = lax.all_to_all(
        pieces, ("gossip", "shard"), split_axis=0, concat_axis=0, axis_index_groups=planes, tiled=True
    )
    outgoing = mix(sid, gid, step, cycle_order, received)
    arrived = lax.all_to_all(outgoing, "gossip", split_axis=0, concat_axis=0, tiled=True)
    new_params, new_weight = finish(ps_weight, own, arrived)
    return (grad_in[None], new_params[None], new_weight)


def solution(mesh):
    placed = (
        P("gossip", "shard", None),
        P("gossip", "shard", None),
        P("gossip", "shard", None),
        P("gossip"),
        P(),
        P(),
    )
    return jax.shard_map(
        body,
        mesh=mesh,
        in_specs=placed,
        out_specs=(P("gossip", "shard", None), P("gossip", "shard", None), P("gossip")),
        check_vma=False,
    )
```

```python
import functools

import jax
import jax.numpy as jnp
from jax import lax
from jax.experimental import pallas as pl
from jax.experimental.pallas import tpu as pltpu
from jax.sharding import PartitionSpec as P

LEARN_RATE = 0.5
NX, NY = 4, 4
ROWS = 64
LANES = 1024
HALF = 512


def mask_of(core, j):
    return (0, 1 + 2 * core, 3 - 2 * core, 2)[j]


def place(sid):
    return sid // 8, (sid // 2) % 4, sid % 2


def pairs(axis, stage):
    out = []
    for s in range(2 * NX * NY):
        x, y, c = s // 8, (s // 2) % 4, s % 2
        if axis == "core":
            c ^= 1
        elif axis == "x":
            x ^= mask_of(c, stage)
        else:
            y ^= mask_of(c, stage)
        out.append((s, (x * NY + y) * 2 + c))
    return out


def send(v, axis, stage=0):
    return lax.ppermute(v, "shard", pairs(axis, stage))


def vmem():
    return pl.BlockSpec(memory_space=pltpu.VMEM)


def smem():
    return pl.BlockSpec(memory_space=pltpu.SMEM)


def params(mib):
    return pltpu.CompilerParams(vmem_limit_bytes=mib << 20)


def split_kernel(sid_ref, x_ref, xp_ref, own_ref, other_ref, wide):
    cx, _, core = place(sid_ref[0])
    rows, width = x_ref.shape
    main = width // 128 * 128
    wide[:, main:] = jnp.zeros((rows, wide.shape[1] - main), wide.dtype)
    for block, src in enumerate((x_ref, xp_ref)):
        wide[:, :main] = src[:, :main]
        wide[:, main:width] = src[:, main:]
        at_rows = slice(rows * block, rows * block + rows)
        for c, out_ref in ((core, own_ref), (1 - core, other_ref)):
            for jx in range(NX):
                col = pl.multiple_of((cx ^ mask_of(c, jx)) * 512, 512)
                for q in range(2):
                    t = wide[:, pl.ds(pl.multiple_of(col + 256 * q, 256), 256)].astype(jnp.float32)
                    t0, t1 = t[:, :128], t[:, 128:]
                    low = lax.broadcasted_iota(jnp.int32, t0.shape, 1) < 64
                    even = jnp.where(low, t0, pltpu.roll(t1, 64, 1))
                    odd = jnp.where(low, pltpu.roll(t0, 64, 1), t1)
                    at = slice(256 * jx + 128 * q, 256 * jx + 128 * q + 128)
                    out_ref[at_rows, at] = jnp.where(c == 0, even, odd).astype(jnp.bfloat16)


def split_by_core(sid, x, x_other):
    rows = x.shape[0]
    half = jax.ShapeDtypeStruct((2 * rows, NX * NY * ROWS), jnp.bfloat16)
    return pl.pallas_call(
        split_kernel,
        in_specs=[smem(), vmem(), vmem()],
        out_specs=[vmem(), vmem()],
        out_shape=[half, half],
        scratch_shapes=[pltpu.VMEM((rows, 2 * NX * NY * ROWS), jnp.bfloat16)],
        compiler_params=params(16),
        cost_estimate=pl.CostEstimate(flops=rows * 4096 * 4, bytes_accessed=rows * 16384, transcendentals=0),
        name="split_by_core",
    )(sid, x, x_other)


def forward_kernel(xk_ref, xs_ref, up_ref, upp_ref, a0, a1, b0, b1, d_ref):
    rows, cols = up_ref.shape
    for block, u_ref in enumerate((up_ref, upp_ref)):
        at = slice(rows * block, rows * block + rows)
        for n in range(2):
            out = slice(HALF * n, HALF * n + HALF)
            z = None
            for x_ref, refs in ((xk_ref, (a0, a1)), (xs_ref, (b0, b1))):
                for i, ref in enumerate(refs):
                    term = jnp.dot(
                        x_ref[at, 512 * i:512 * i + 512], ref[:, out], preferred_element_type=jnp.float32
                    )
                    z = term if z is None else z + term
            width = min(HALF, cols - HALF * n)
            z = z[:, :width]
            s = 1.0 / (1.0 + jnp.exp(-z))
            up = u_ref[:, HALF * n:HALF * n + width].astype(jnp.float32)
            d = up * s * (1.0 + z * (1.0 - s))
            if width < HALF:
                d_ref[at, LANES - 128:] = jnp.zeros((rows, 128), jnp.bfloat16)
            d_ref[at, HALF * n:HALF * n + width] = d.astype(jnp.bfloat16)


def forward(xk, xs, up, up_other, a0, a1, b0, b1):
    rows, cols = up.shape
    half = NX * NY * ROWS
    return pl.pallas_call(
        forward_kernel,
        in_specs=[vmem()] * 8,
        out_specs=vmem(),
        out_shape=jax.ShapeDtypeStruct((2 * rows, LANES), jnp.bfloat16),
        compiler_params=params(28),
        cost_estimate=pl.CostEstimate(
            flops=8 * rows * half * cols, bytes_accessed=4 << 20, transcendentals=2 * rows * cols
        ),
        name="forward",
    )(xk, xs, up, up_other, a0, a1, b0, b1)


def back_kernel(width, sid_ref, d_ref, a0, a1, b0, b1, out_ref, wv):
    cx, _, core = place(sid_ref[0])
    rows = out_ref.shape[0]
    for k, src in enumerate((a0, a1, b0, b1)):
        c = core if k < 2 else 1 - core
        for jx in range(2):
            for jy in range(4):
                bx = cx ^ mask_of(c, jx + 2 * (k % 2))
                row = pl.multiple_of(((bx * NY + jy) * 2 + c) * ROWS, ROWS)
                at = (jx * 4 + jy) * ROWS
                wv[pl.ds(row, ROWS), :] = src[at:at + ROWS, :]
    dims = (((1,), (1,)), ((), ()))
    for n in range(4):
        g = lax.dot_general(
            d_ref[:rows], wv[512 * n:512 * n + 512], dims, preferred_element_type=jnp.float32
        )
        take = min(512, width - 512 * n)
        out_ref[:, 512 * n:512 * n + take] = g[:, :take].astype(jnp.bfloat16)


def back(sid, rows, width, d, a0, a1, b0, b1):
    return pl.pallas_call(
        functools.partial(back_kernel, width),
        in_specs=[smem()] + [vmem()] * 5,
        out_specs=vmem(),
        out_shape=jax.ShapeDtypeStruct((rows, width), jnp.bfloat16),
        scratch_shapes=[pltpu.VMEM((2048, LANES), jnp.bfloat16)],
        compiler_params=params(20),
        cost_estimate=pl.CostEstimate(flops=2 * rows * 2048 * LANES, bytes_accessed=8 << 20, transcendentals=0),
        name="back",
    )(sid, d, a0, a1, b0, b1)


def partial_kernel(first, part, x_ref, d_ref, out_ref):
    dims = (((0,), (0,)), ((), ()))
    x = x_ref[:, 256 * first:256 * first + 512]
    d = d_ref[:, HALF * part:HALF * part + HALF]
    out_ref[...] = lax.dot_general(x, d, dims, preferred_element_type=jnp.float32).astype(jnp.bfloat16)


def partial(first, part, x, d):
    rows = d.shape[0]
    return pl.pallas_call(
        functools.partial(partial_kernel, first, part),
        in_specs=[vmem()] * 2,
        out_specs=vmem(),
        out_shape=jax.ShapeDtypeStruct((512, HALF), jnp.bfloat16),
        compiler_params=params(16),
        cost_estimate=pl.CostEstimate(flops=2 * rows * 512 * HALF, bytes_accessed=2 << 20, transcendentals=0),
        name="partial_%d_%d" % (first, part),
    )(x, d)


def pack_kernel(scale, sid_ref, w_ref, p_ref, ka_ref, ga_ref, kb_ref, gb_ref, own_ref, pack_ref):
    _, cy, _ = place(sid_ref[0])
    rows, cols = p_ref.shape
    tail = cols - 7 * 128
    w = jnp.full((32, 128), w_ref[0], jnp.float32)
    hi = w.astype(jnp.bfloat16).astype(jnp.float32)
    lane = lax.broadcasted_iota(jnp.int32, (32, 128), 1)
    spare = jnp.where(lane == 126, hi, jnp.where(lane == 127, w - hi, 0.0)).astype(jnp.bfloat16)
    for y in range(NY):
        at = slice(ROWS * y, ROWS * y + ROWS)
        v = jnp.concatenate(
            [
                scale * (keep_ref[at].astype(jnp.float32) + got_ref[at].astype(jnp.float32))
                for keep_ref, got_ref in ((ka_ref, ga_ref), (kb_ref, gb_ref))
            ],
            axis=1,
        )
        for h in range(2):
            for j in range(8):
                pack_ref[y * 16 + 8 * h + j] = v[32 * h:32 * h + 32, 128 * j:128 * j + 128].astype(jnp.bfloat16)
    at = pl.ds(pl.multiple_of(cy * ROWS, ROWS), ROWS)
    v = jnp.concatenate(
        [
            scale * (keep_ref[at].astype(jnp.float32) + got_ref[at].astype(jnp.float32))
            for keep_ref, got_ref in ((ka_ref, ga_ref), (kb_ref, gb_ref))
        ],
        axis=1,
    )
    own = p_ref[...] + v[:, :cols]
    own_ref[...] = own
    for h in range(2):
        for j in range(8):
            to = cy * 16 + 8 * h + j
            if j == 7:
                pack_ref[to] = spare
                pack_ref[to, :, :tail] = own[32 * h:32 * h + 32, 896:].astype(jnp.bfloat16)
            else:
                pack_ref[to] = own[32 * h:32 * h + 32, 128 * j:128 * j + 128].astype(jnp.bfloat16)


def pack(scale, sid, weight, own, *sums):
    return pl.pallas_call(
        functools.partial(pack_kernel, scale),
        in_specs=[smem(), smem()] + [vmem()] * 5,
        out_specs=[vmem(), vmem()],
        out_shape=[
            jax.ShapeDtypeStruct(own.shape, jnp.float32),
            jax.ShapeDtypeStruct((64, 32, 128), jnp.bfloat16),
        ],
        compiler_params=params(8),
        cost_estimate=pl.CostEstimate(flops=1 << 20, bytes_accessed=2 << 20, transcendentals=0),
        name="pack",
    )(sid, weight, own, *sums)


def mix_kernel(sid_ref, gid_ref, step_ref, order_ref, in_ref, out_ref, total):
    _, cy, _ = place(sid_ref[0])
    for g in range(16):
        t = in_ref[g].astype(jnp.float32)
        for y in range(1, NY):
            t = t + in_ref[16 * y + g].astype(jnp.float32)
        total[g] = t
    lane = lax.broadcasted_iota(jnp.int32, (32, 128), 1)
    spare = (lane >= 126) & (gid_ref[0] % 8 == 7)
    distance = 1 << lax.rem(step_ref[0], 4)
    for p in range(16):
        m = order_ref[p]
        source = total[order_ref[(p - distance + 16) % 16]]
        rest = total[m] - in_ref[16 * cy + m].astype(jnp.float32)
        out_ref[m] = jnp.where(spare, source, 0.5 * (source + rest)).astype(jnp.bfloat16)


def mix(sid, gid, step, order, got):
    return pl.pallas_call(
        mix_kernel,
        in_specs=[smem()] * 4 + [vmem()],
        out_specs=vmem(),
        out_shape=jax.ShapeDtypeStruct((16, 32, 128), jnp.bfloat16),
        scratch_shapes=[pltpu.VMEM((16, 32, 128), jnp.float32)],
        compiler_params=params(8),
        cost_estimate=pl.CostEstimate(flops=1 << 20, bytes_accessed=1 << 20, transcendentals=0),
        name="mix",
    )(sid, gid, step, order, got)


def finish_kernel(w_ref, own_ref, got_ref, new_ref, new_w_ref):
    rows, cols = own_ref.shape
    for h in range(2):
        for j in range(8):
            width = min(128, cols - 128 * j)
            at = (slice(32 * h, 32 * h + 32), slice(128 * j, 128 * j + width))
            new_ref[at] = 0.5 * own_ref[at] + got_ref[8 * h + j].astype(jnp.float32)[:, :width]
    last = got_ref[7].astype(jnp.float32)
    lane = lax.broadcasted_iota(jnp.int32, last.shape, 1)
    row = lax.broadcasted_iota(jnp.int32, last.shape, 0)
    source_w = jnp.sum(jnp.where((lane >= 126) & (row == 0), last, 0.0))
    new_w_ref[0] = 0.5 * w_ref[0] + 0.5 * source_w


def finish(weight, own, got):
    return pl.pallas_call(
        finish_kernel,
        in_specs=[smem(), vmem(), vmem()],
        out_specs=[vmem(), smem()],
        out_shape=[
            jax.ShapeDtypeStruct(own.shape, jnp.float32),
            jax.ShapeDtypeStruct((1,), jnp.float32),
        ],
        compiler_params=params(8),
        name="finish",
    )(weight, own, got)


def add(a, b):
    return (a.astype(jnp.float32) + b.astype(jnp.float32)).astype(jnp.bfloat16)


def halves(a):
    n = a.shape[0] // 2
    return a[:n], a[n:]


def body(inputs, upstream, params, ps_weight, step, cycle_order):
    x_rows = inputs[0]
    up_rows = upstream[0]
    own_shard = params[0]
    n_shard = lax.axis_size("shard")
    n_groups = lax.axis_size("gossip")
    in_width = x_rows.shape[1]
    sid = lax.axis_index("shard").astype(jnp.int32).reshape(1)

    debiased = (own_shard / ps_weight[0]).astype(jnp.bfloat16)
    debiased = jnp.pad(debiased, ((0, 0), (0, LANES - debiased.shape[1])))
    columns = [[(x * NY + y) * 2 + c for y in range(NY)] for x in range(NX) for c in range(2)]
    held = lax.all_gather(debiased, "shard", axis=0, axis_index_groups=columns, tiled=True)
    held, x_rows, up_rows = lax.optimization_barrier((held, x_rows, up_rows))
    held = jnp.concatenate([held, send(held, "x", 1)])
    x_other, up_other = send(x_rows, "core"), send(up_rows, "core")
    far = send(held, "x", 2)
    other_held = send(held, "core")
    x_own, x_far = split_by_core(sid, x_rows, x_other)
    far, x_own, x_far, up_other = lax.optimization_barrier((far, x_own, x_far, up_other))
    other_far = send(far, "core")
    weights = (held, far, other_held, other_far)

    d_pre = forward(x_own, x_far, up_rows, up_other, *weights)
    got = [send(partial(2, i, x_own, d_pre), "x", 2) for i in range(2)]
    keep = [partial(0, i, x_own, d_pre) for i in range(2)]
    sums = []
    for i in range(2):
        (k0, k1), (g0, g1) = halves(keep[i]), halves(got[i])
        sums.extend([add(k0, g0), send(add(k1, g1), "x", 1)])
    grad_in = back(sid, x_rows.shape[0], in_width, d_pre, *weights)
    sums[3], grad_in = lax.optimization_barrier((sums[3], grad_in))

    tokens = x_rows.shape[0] * n_shard
    gid = lax.axis_index("gossip").astype(jnp.int32).reshape(1)
    own, pieces = pack(-LEARN_RATE / tokens, sid, ps_weight, own_shard, *sums)
    planes = [
        [g * n_shard + (x * NY + y) * 2 + c for y in range(NY) for g in range(n_groups)]
        for x in range(NX) for c in range(2)
    ]
    received = lax.all_to_all(
        pieces, ("gossip", "shard"), split_axis=0, concat_axis=0, axis_index_groups=planes, tiled=True
    )
    outgoing = mix(sid, gid, step, cycle_order, received)
    arrived = lax.all_to_all(outgoing, "gossip", split_axis=0, concat_axis=0, tiled=True)
    new_params, new_weight = finish(ps_weight, own, arrived)
    return (grad_in[None], new_params[None], new_weight)


def solution(mesh):
    placed = (
        P("gossip", "shard", None),
        P("gossip", "shard", None),
        P("gossip", "shard", None),
        P("gossip"),
        P(),
        P(),
    )
    return jax.shard_map(
        body,
        mesh=mesh,
        in_specs=placed,
        out_specs=(P("gossip", "shard", None), P("gossip", "shard", None), P("gossip")),
        check_vma=False,
    )
```

```python
import functools

import jax
import jax.numpy as jnp
from jax import lax
from jax.experimental import pallas as pl
from jax.experimental.pallas import tpu as pltpu
from jax.sharding import PartitionSpec as P


LEARN_RATE = 0.5
NX, NY = 4, 4
ROWS = 64
LANES = 1024
HALF = 512


def mask_of(core, j):
    return (0, 1 + 2 * core, 3 - 2 * core, 2)[j]


def place(sid):
    return sid // 8, (sid // 2) % 4, sid % 2


def pairs(axis, stage):
    out = []
    for s in range(2 * NX * NY):
        x, y, c = s // 8, (s // 2) % 4, s % 2
        if axis == "core":
            c ^= 1
        elif axis == "x":
            x ^= mask_of(c, stage)
        else:
            y ^= mask_of(c, stage)
        out.append((s, (x * NY + y) * 2 + c))
    return out


def send(v, axis, stage=0):
    return lax.ppermute(v, "shard", pairs(axis, stage))


def vmem():
    return pl.BlockSpec(memory_space=pltpu.VMEM)


def smem():
    return pl.BlockSpec(memory_space=pltpu.SMEM)


def params(mib):
    return pltpu.CompilerParams(vmem_limit_bytes=mib << 20)


def split_kernel(sid_ref, x_ref, own_ref, other_ref, wide):
    cx, _, core = place(sid_ref[0])
    rows, width = x_ref.shape
    main = width // 128 * 128
    wide[:, main:] = jnp.zeros((rows, wide.shape[1] - main), wide.dtype)
    wide[:, :main] = x_ref[:, :main]
    wide[:, main:width] = x_ref[:, main:]
    for c, out_ref in ((core, own_ref), (1 - core, other_ref)):
        for jx in range(NX):
            col = pl.multiple_of((cx ^ mask_of(c, jx)) * 512, 512)
            for q in range(2):
                t = wide[:, pl.ds(pl.multiple_of(col + 256 * q, 256), 256)].astype(jnp.float32)
                t0, t1 = t[:, :128], t[:, 128:]
                low = lax.broadcasted_iota(jnp.int32, t0.shape, 1) < 64
                even = jnp.where(low, t0, pltpu.roll(t1, 64, 1))
                odd = jnp.where(low, pltpu.roll(t0, 64, 1), t1)
                at = slice(256 * jx + 128 * q, 256 * jx + 128 * q + 128)
                out_ref[:, at] = jnp.where(c == 0, even, odd).astype(jnp.bfloat16)


def split_by_core(sid, x):
    rows = x.shape[0]
    half = jax.ShapeDtypeStruct((rows, NX * NY * ROWS), jnp.bfloat16)
    return pl.pallas_call(
        split_kernel,
        in_specs=[smem(), vmem()],
        out_specs=[vmem(), vmem()],
        out_shape=[half, half],
        scratch_shapes=[pltpu.VMEM((rows, 2 * NX * NY * ROWS), jnp.bfloat16)],
        compiler_params=params(16),
        cost_estimate=pl.CostEstimate(flops=rows * 2048 * 4, bytes_accessed=rows * 8192, transcendentals=0),
    )(sid, x)


def product_kernel(terms, first, *refs):
    xs, ws, rest = refs[:2 * terms], refs[2 * terms:3 * terms], refs[3 * terms:]
    z_ref, out_ref = (None, rest[0]) if len(rest) == 1 else rest
    rows = xs[0].shape[0]
    for block in range(2):
        at = slice(rows * block, rows * block + rows)
        for n in range(2):
            out = slice(HALF * n, HALF * n + HALF)
            z = None if z_ref is None else z_ref[at, out]
            for i in range(terms):
                x = xs[2 * i + block][:, first:first + 512]
                term = jnp.dot(x, ws[i][:, out], preferred_element_type=jnp.float32)
                z = term if z is None else z + term
            out_ref[at, out] = z


def product(first, xs, ws, z=None):
    rows = xs[0].shape[0]
    terms = len(ws)
    ops = (*xs, *ws) if z is None else (*xs, *ws, z)
    return pl.pallas_call(
        functools.partial(product_kernel, terms, first),
        in_specs=[vmem()] * len(ops),
        out_specs=vmem(),
        out_shape=jax.ShapeDtypeStruct((2 * rows, LANES), jnp.float32),
        compiler_params=params(20),
        cost_estimate=pl.CostEstimate(
            flops=4 * terms * rows * 512 * LANES, bytes_accessed=4 << 20, transcendentals=0
        ),
    )(*ops)


def forward_kernel(x_ref, xp_ref, w_ref, z_ref, up_ref, upp_ref, d_ref):
    rows, cols = up_ref.shape
    for block, (x, u_ref) in enumerate(((x_ref, up_ref), (xp_ref, upp_ref))):
        at = slice(rows * block, rows * block + rows)
        for n in range(2):
            out = slice(HALF * n, HALF * n + HALF)
            z = z_ref[at, out] + jnp.dot(x[:, 512:], w_ref[:, out], preferred_element_type=jnp.float32)
            width = min(HALF, cols - HALF * n)
            z = z[:, :width]
            s = 1.0 / (1.0 + jnp.exp(-z))
            up = u_ref[:, HALF * n:HALF * n + width].astype(jnp.float32)
            d = up * s * (1.0 + z * (1.0 - s))
            if width < HALF:
                d_ref[at, LANES - 128:] = jnp.zeros((rows, 128), jnp.bfloat16)
            d_ref[at, HALF * n:HALF * n + width] = d.astype(jnp.bfloat16)


def forward(x, x_other, w, z, up, up_other):
    rows, cols = up.shape
    return pl.pallas_call(
        forward_kernel,
        in_specs=[vmem()] * 6,
        out_specs=vmem(),
        out_shape=jax.ShapeDtypeStruct((2 * rows, LANES), jnp.bfloat16),
        compiler_params=params(24),
        cost_estimate=pl.CostEstimate(
            flops=4 * rows * 512 * cols, bytes_accessed=4 << 20, transcendentals=2 * rows * cols
        ),
        name="forward",
    )(x, x_other, w, z, up, up_other)


def back_kernel(width, sid_ref, d_ref, a0, a1, b0, b1, out_ref, wv):
    cx, _, core = place(sid_ref[0])
    rows = out_ref.shape[0]
    for k, src in enumerate((a0, a1, b0, b1)):
        c = core if k < 2 else 1 - core
        for jx in range(2):
            for jy in range(4):
                bx = cx ^ mask_of(c, jx + 2 * (k % 2))
                row = pl.multiple_of(((bx * NY + jy) * 2 + c) * ROWS, ROWS)
                at = (jx * 4 + jy) * ROWS
                wv[pl.ds(row, ROWS), :] = src[at:at + ROWS, :]
    dims = (((1,), (1,)), ((), ()))
    for n in range(4):
        g = lax.dot_general(
            d_ref[:rows], wv[512 * n:512 * n + 512], dims, preferred_element_type=jnp.float32
        )
        take = min(512, width - 512 * n)
        out_ref[:, 512 * n:512 * n + take] = g[:, :take].astype(jnp.bfloat16)


def back(sid, rows, width, d, a0, a1, b0, b1):
    return pl.pallas_call(
        functools.partial(back_kernel, width),
        in_specs=[smem()] + [vmem()] * 5,
        out_specs=vmem(),
        out_shape=jax.ShapeDtypeStruct((rows, width), jnp.bfloat16),
        scratch_shapes=[pltpu.VMEM((2048, LANES), jnp.bfloat16)],
        compiler_params=params(20),
        cost_estimate=pl.CostEstimate(flops=2 * rows * 2048 * LANES, bytes_accessed=8 << 20, transcendentals=0),
        name="back",
    )(sid, d, a0, a1, b0, b1)


def partial_kernel(first, part, x_ref, xp_ref, d_ref, out_ref):
    dims = (((0,), (0,)), ((), ()))
    rows = x_ref.shape[0]
    columns = slice(256 * first, 256 * first + 512)
    out = slice(HALF * part, HALF * part + HALF)
    r = lax.dot_general(x_ref[:, columns], d_ref[:rows, out], dims, preferred_element_type=jnp.float32)
    r = r + lax.dot_general(xp_ref[:, columns], d_ref[rows:, out], dims, preferred_element_type=jnp.float32)
    out_ref[...] = r.astype(jnp.bfloat16)


def partial(first, part, x, x_other, d):
    rows = d.shape[0]
    return pl.pallas_call(
        functools.partial(partial_kernel, first, part),
        in_specs=[vmem()] * 3,
        out_specs=vmem(),
        out_shape=jax.ShapeDtypeStruct((512, HALF), jnp.bfloat16),
        compiler_params=params(16),
        cost_estimate=pl.CostEstimate(flops=2 * rows * 512 * HALF, bytes_accessed=2 << 20, transcendentals=0),
    )(x, x_other, d)


def pack_kernel(scale, sid_ref, w_ref, p_ref, ka_ref, ga_ref, kb_ref, gb_ref, own_ref, pack_ref):
    _, cy, _ = place(sid_ref[0])
    _, cols = p_ref.shape
    tail = cols - 7 * 128
    w = jnp.full((32, 128), w_ref[0], jnp.float32)
    hi = w.astype(jnp.bfloat16).astype(jnp.float32)
    lane = lax.broadcasted_iota(jnp.int32, (32, 128), 1)
    spare = jnp.where(lane == 126, hi, jnp.where(lane == 127, w - hi, 0.0)).astype(jnp.bfloat16)
    for y in range(NY):
        at = slice(ROWS * y, ROWS * y + ROWS)
        v = jnp.concatenate(
            [
                scale * (keep_ref[at].astype(jnp.float32) + got_ref[at].astype(jnp.float32))
                for keep_ref, got_ref in ((ka_ref, ga_ref), (kb_ref, gb_ref))
            ],
            axis=1,
        )
        for h in range(2):
            for j in range(8):
                pack_ref[y * 16 + 8 * h + j] = v[32 * h:32 * h + 32, 128 * j:128 * j + 128].astype(jnp.bfloat16)
    at = pl.ds(pl.multiple_of(cy * ROWS, ROWS), ROWS)
    v = jnp.concatenate(
        [
            scale * (keep_ref[at].astype(jnp.float32) + got_ref[at].astype(jnp.float32))
            for keep_ref, got_ref in ((ka_ref, ga_ref), (kb_ref, gb_ref))
        ],
        axis=1,
    )
    own = p_ref[...] + v[:, :cols]
    own_ref[...] = own
    for h in range(2):
        for j in range(8):
            to = cy * 16 + 8 * h + j
            if j == 7:
                pack_ref[to] = spare
                pack_ref[to, :, :tail] = own[32 * h:32 * h + 32, 896:].astype(jnp.bfloat16)
            else:
                pack_ref[to] = own[32 * h:32 * h + 32, 128 * j:128 * j + 128].astype(jnp.bfloat16)


def pack(scale, sid, weight, own, *sums):
    return pl.pallas_call(
        functools.partial(pack_kernel, scale),
        in_specs=[smem(), smem()] + [vmem()] * 5,
        out_specs=[vmem(), vmem()],
        out_shape=[
            jax.ShapeDtypeStruct(own.shape, jnp.float32),
            jax.ShapeDtypeStruct((64, 32, 128), jnp.bfloat16),
        ],
        compiler_params=params(8),
        cost_estimate=pl.CostEstimate(flops=1 << 20, bytes_accessed=2 << 20, transcendentals=0),
        name="pack",
    )(sid, weight, own, *sums)


def mix_kernel(sid_ref, gid_ref, step_ref, order_ref, in_ref, out_ref, total):
    _, cy, _ = place(sid_ref[0])
    for g in range(16):
        t = in_ref[g].astype(jnp.float32)
        for y in range(1, NY):
            t = t + in_ref[16 * y + g].astype(jnp.float32)
        total[g] = t
    lane = lax.broadcasted_iota(jnp.int32, (32, 128), 1)
    spare = (lane >= 126) & (gid_ref[0] % 8 == 7)
    distance = 1 << lax.rem(step_ref[0], 4)
    for p in range(16):
        m = order_ref[p]
        source = total[order_ref[(p - distance + 16) % 16]]
        rest = total[m] - in_ref[16 * cy + m].astype(jnp.float32)
        out_ref[m] = jnp.where(spare, source, 0.5 * (source + rest)).astype(jnp.bfloat16)


def mix(sid, gid, step, order, got):
    return pl.pallas_call(
        mix_kernel,
        in_specs=[smem()] * 4 + [vmem()],
        out_specs=vmem(),
        out_shape=jax.ShapeDtypeStruct((16, 32, 128), jnp.bfloat16),
        scratch_shapes=[pltpu.VMEM((16, 32, 128), jnp.float32)],
        compiler_params=params(8),
        cost_estimate=pl.CostEstimate(flops=1 << 20, bytes_accessed=1 << 20, transcendentals=0),
        name="mix",
    )(sid, gid, step, order, got)


def finish_kernel(w_ref, own_ref, got_ref, new_ref, new_w_ref):
    _, cols = own_ref.shape
    for h in range(2):
        for j in range(8):
            width = min(128, cols - 128 * j)
            at = (slice(32 * h, 32 * h + 32), slice(128 * j, 128 * j + width))
            new_ref[at] = 0.5 * own_ref[at] + got_ref[8 * h + j].astype(jnp.float32)[:, :width]
    last = got_ref[7].astype(jnp.float32)
    lane = lax.broadcasted_iota(jnp.int32, last.shape, 1)
    row = lax.broadcasted_iota(jnp.int32, last.shape, 0)
    source_w = jnp.sum(jnp.where((lane >= 126) & (row == 0), last, 0.0))
    new_w_ref[0] = 0.5 * w_ref[0] + 0.5 * source_w


def finish(weight, own, got):
    return pl.pallas_call(
        finish_kernel,
        in_specs=[smem(), vmem(), vmem()],
        out_specs=[vmem(), smem()],
        out_shape=[
            jax.ShapeDtypeStruct(own.shape, jnp.float32),
            jax.ShapeDtypeStruct((1,), jnp.float32),
        ],
        compiler_params=params(8),
        name="finish",
    )(weight, own, got)


def add(a, b):
    return (a.astype(jnp.float32) + b.astype(jnp.float32)).astype(jnp.bfloat16)


def halves(a):
    n = a.shape[0] // 2
    return a[:n], a[n:]


def body(inputs, upstream, params, ps_weight, step, cycle_order):
    x_rows = inputs[0]
    up_rows = upstream[0]
    own_shard = params[0]
    n_shard = lax.axis_size("shard")
    n_groups = lax.axis_size("gossip")
    in_width = x_rows.shape[1]
    sid = lax.axis_index("shard").astype(jnp.int32).reshape(1)

    debiased = (own_shard / ps_weight[0]).astype(jnp.bfloat16)
    debiased = jnp.pad(debiased, ((0, 0), (0, LANES - debiased.shape[1])))
    columns = [[(x * NY + y) * 2 + c for y in range(NY)] for x in range(NX) for c in range(2)]
    held = lax.all_gather(debiased, "shard", axis=0, axis_index_groups=columns, tiled=True)
    held, x_rows, up_rows = lax.optimization_barrier((held, x_rows, up_rows))
    got = send(held, "x", 1)
    x_other = send(x_rows, "core")
    xa, xb = split_by_core(sid, x_rows)
    got, xa, xb = lax.optimization_barrier((got, xa, xb))
    held = jnp.concatenate([held, got])
    up_other = send(up_rows, "core")
    far = send(held, "x", 2)
    other_held = send(held, "core")
    ya, yb = split_by_core(sid, x_other)
    z = product(0, (xa, ya, xb, yb), (held, other_held))
    far, z, up_other = lax.optimization_barrier((far, z, up_other))
    other_far = send(far, "core")
    weights = (held, far, other_held, other_far)
    z = product(512, (xa, ya), (far,), z)
    d_pre = forward(xb, yb, other_far, z, up_rows, up_other)
    got = [send(partial(2, i, xa, ya, d_pre), "x", 2) for i in range(2)]
    keep = [partial(0, i, xa, ya, d_pre) for i in range(2)]
    sums = []
    for i in range(2):
        (k0, k1), (g0, g1) = halves(keep[i]), halves(got[i])
        sums.extend([add(k0, g0), send(add(k1, g1), "x", 1)])
    grad_in = back(sid, x_rows.shape[0], in_width, d_pre, *weights)
    sums[3], grad_in = lax.optimization_barrier((sums[3], grad_in))

    tokens = x_rows.shape[0] * n_shard
    gid = lax.axis_index("gossip").astype(jnp.int32).reshape(1)
    own, pieces = pack(-LEARN_RATE / tokens, sid, ps_weight, own_shard, *sums)
    planes = [
        [g * n_shard + (x * NY + y) * 2 + c for y in range(NY) for g in range(n_groups)]
        for x in range(NX) for c in range(2)
    ]
    received = lax.all_to_all(
        pieces, ("gossip", "shard"), split_axis=0, concat_axis=0, axis_index_groups=planes, tiled=True
    )
    outgoing = mix(sid, gid, step, cycle_order, received)
    arrived = lax.all_to_all(outgoing, "gossip", split_axis=0, concat_axis=0, tiled=True)
    new_params, new_weight = finish(ps_weight, own, arrived)
    return (grad_in[None], new_params[None], new_weight)


def solution(mesh):
    placed = (
        P("gossip", "shard", None),
        P("gossip", "shard", None),
        P("gossip", "shard", None),
        P("gossip"),
        P(),
        P(),
    )

    return jax.shard_map(
        body,
        mesh=mesh,
        in_specs=placed,
        out_specs=(P("gossip", "shard", None), P("gossip", "shard", None), P("gossip")),
        check_vma=False,
    )
```

```python
import functools

import jax
import jax.numpy as jnp
from jax import lax
from jax.experimental import pallas as pl
from jax.experimental.pallas import tpu as pltpu
from jax.sharding import PartitionSpec as P


LEARN_RATE = 0.5
NX, NY = 4, 4
ROWS = 64
LANES = 1024
HALF = 512


def mask_of(core, j):
    return (0, 1 + 2 * core, 3 - 2 * core, 2)[j]


def place(sid):
    return sid // 8, (sid // 2) % 4, sid % 2


def pairs(axis, stage):
    out = []
    for s in range(2 * NX * NY):
        x, y, c = s // 8, (s // 2) % 4, s % 2
        if axis == "core":
            c ^= 1
        elif axis == "x":
            x ^= mask_of(c, stage)
        else:
            y ^= mask_of(c, stage)
        out.append((s, (x * NY + y) * 2 + c))
    return out


def send(v, axis, stage=0):
    return lax.ppermute(v, "shard", pairs(axis, stage))


def vmem():
    return pl.BlockSpec(memory_space=pltpu.VMEM)


def smem():
    return pl.BlockSpec(memory_space=pltpu.SMEM)


def params(mib):
    return pltpu.CompilerParams(vmem_limit_bytes=mib << 20)


def split_kernel(sid_ref, x_ref, own_ref, other_ref, wide):
    cx, _, core = place(sid_ref[0])
    rows, width = x_ref.shape
    main = width // 128 * 128
    wide[:, main:] = jnp.zeros((rows, wide.shape[1] - main), wide.dtype)
    wide[:, :main] = x_ref[:, :main]
    wide[:, main:width] = x_ref[:, main:]
    for c, out_ref in ((core, own_ref), (1 - core, other_ref)):
        for jx in range(NX):
            col = pl.multiple_of((cx ^ mask_of(c, jx)) * 512, 512)
            for q in range(2):
                t = wide[:, pl.ds(pl.multiple_of(col + 256 * q, 256), 256)].astype(jnp.float32)
                t0, t1 = t[:, :128], t[:, 128:]
                low = lax.broadcasted_iota(jnp.int32, t0.shape, 1) < 64
                even = jnp.where(low, t0, pltpu.roll(t1, 64, 1))
                odd = jnp.where(low, pltpu.roll(t0, 64, 1), t1)
                at = slice(256 * jx + 128 * q, 256 * jx + 128 * q + 128)
                out_ref[:, at] = jnp.where(c == 0, even, odd).astype(jnp.bfloat16)


def split_by_core(sid, x):
    rows = x.shape[0]
    half = jax.ShapeDtypeStruct((rows, NX * NY * ROWS), jnp.bfloat16)
    return pl.pallas_call(
        split_kernel,
        in_specs=[smem(), vmem()],
        out_specs=[vmem(), vmem()],
        out_shape=[half, half],
        scratch_shapes=[pltpu.VMEM((rows, 2 * NX * NY * ROWS), jnp.bfloat16)],
        compiler_params=params(16),
        cost_estimate=pl.CostEstimate(flops=rows * 2048 * 4, bytes_accessed=rows * 8192, transcendentals=0),
    )(sid, x)


def product_kernel(xa_ref, ya_ref, xb_ref, yb_ref, wa_ref, wb_ref, z_ref):
    rows = xa_ref.shape[0]
    for block, (own, other) in enumerate(((xa_ref, xb_ref), (ya_ref, yb_ref))):
        at = slice(rows * block, rows * block + rows)
        for n in range(2):
            out = slice(HALF * n, HALF * n + HALF)
            z = jnp.dot(own[:, :512], wa_ref[:, out], preferred_element_type=jnp.float32)
            z_ref[at, out] = z + jnp.dot(other[:, :512], wb_ref[:, out], preferred_element_type=jnp.float32)


def product(xa, ya, xb, yb, wa, wb):
    rows = xa.shape[0]
    return pl.pallas_call(
        product_kernel,
        in_specs=[vmem()] * 6,
        out_specs=vmem(),
        out_shape=jax.ShapeDtypeStruct((2 * rows, LANES), jnp.float32),
        compiler_params=params(20),
        cost_estimate=pl.CostEstimate(flops=8 * rows * 512 * LANES, bytes_accessed=4 << 20, transcendentals=0),
        name="product_held",
    )(xa, ya, xb, yb, wa, wb)


def product_far_kernel(part, x_ref, y_ref, w_ref, z_ref, out_ref):
    rows = x_ref.shape[0]
    columns = slice(HALF * part, HALF * part + HALF)
    for block, x in enumerate((x_ref, y_ref)):
        at = slice(rows * block, rows * block + rows)
        out_ref[at] = z_ref[at, columns] + jnp.dot(
            x[:, 512:], w_ref[...], preferred_element_type=jnp.float32
        )


def product_far(part, x, y, w, z):
    rows = x.shape[0]
    return pl.pallas_call(
        functools.partial(product_far_kernel, part),
        in_specs=[vmem()] * 4,
        out_specs=vmem(),
        out_shape=jax.ShapeDtypeStruct((2 * rows, HALF), jnp.float32),
        compiler_params=params(16),
        cost_estimate=pl.CostEstimate(flops=4 * rows * 512 * HALF, bytes_accessed=2 << 20, transcendentals=0),
    )(x, y, w, z)


def forward_kernel(part, x_ref, y_ref, w_ref, z_ref, up_ref, upp_ref, d_ref):
    rows, cols = up_ref.shape
    first = HALF * part
    width = min(HALF, cols - first)
    if width < HALF:
        d_ref[:, HALF - 128:] = jnp.zeros((2 * rows, 128), jnp.bfloat16)
    for block, (x, u_ref) in enumerate(((x_ref, up_ref), (y_ref, upp_ref))):
        at = slice(rows * block, rows * block + rows)
        z = z_ref[at] + jnp.dot(x[:, 512:], w_ref[...], preferred_element_type=jnp.float32)
        z = z[:, :width]
        s = 1.0 / (1.0 + jnp.exp(-z))
        d = u_ref[:, first:first + width].astype(jnp.float32) * s * (1.0 + z * (1.0 - s))
        d_ref[at, :width] = d.astype(jnp.bfloat16)


def forward(part, x, y, w, z, up, up_other):
    rows = up.shape[0]
    return pl.pallas_call(
        functools.partial(forward_kernel, part),
        in_specs=[vmem()] * 6,
        out_specs=vmem(),
        out_shape=jax.ShapeDtypeStruct((2 * rows, HALF), jnp.bfloat16),
        compiler_params=params(20),
        cost_estimate=pl.CostEstimate(
            flops=4 * rows * 512 * HALF, bytes_accessed=3 << 20, transcendentals=2 * rows * HALF
        ),
    )(x, y, w, z, up, up_other)


def back_kernel(width, sid_ref, da_ref, db_ref, h0, fa0, fb0, h1, fa1, fb1, out_ref, wv):
    cx, _, core = place(sid_ref[0])
    rows = out_ref.shape[0]
    for c, held, fars in ((core, h0, (fa0, fb0)), (1 - core, h1, (fa1, fb1))):
        for j in range(NX):
            bx = cx ^ mask_of(c, j)
            for by in range(NY):
                to = pl.ds(pl.multiple_of(((bx * NY + by) * 2 + c) * ROWS, ROWS), ROWS)
                at = ((j % 2) * NY + by) * ROWS
                if j < 2:
                    wv[to, :] = held[at:at + ROWS, :]
                else:
                    for i, far in enumerate(fars):
                        wv[to, HALF * i:HALF * i + HALF] = far[at:at + ROWS, :]
    dims = (((1,), (1,)), ((), ()))
    for n in range(4):
        at = slice(512 * n, 512 * n + 512)
        g = lax.dot_general(da_ref[:rows], wv[at, :HALF], dims, preferred_element_type=jnp.float32)
        g = g + lax.dot_general(db_ref[:rows], wv[at, HALF:], dims, preferred_element_type=jnp.float32)
        take = min(512, width - 512 * n)
        out_ref[:, 512 * n:512 * n + take] = g[:, :take].astype(jnp.bfloat16)


def back(sid, rows, width, d, pieces):
    return pl.pallas_call(
        functools.partial(back_kernel, width),
        in_specs=[smem()] + [vmem()] * 8,
        out_specs=vmem(),
        out_shape=jax.ShapeDtypeStruct((rows, width), jnp.bfloat16),
        scratch_shapes=[pltpu.VMEM((2048, LANES), jnp.bfloat16)],
        compiler_params=params(20),
        cost_estimate=pl.CostEstimate(flops=2 * rows * 2048 * LANES, bytes_accessed=8 << 20, transcendentals=0),
        name="back",
    )(sid, *d, *pieces)


def partial_kernel(first, x_ref, xp_ref, d_ref, out_ref):
    dims = (((0,), (0,)), ((), ()))
    rows = x_ref.shape[0]
    columns = slice(256 * first, 256 * first + 512)
    r = lax.dot_general(x_ref[:, columns], d_ref[:rows], dims, preferred_element_type=jnp.float32)
    r = r + lax.dot_general(xp_ref[:, columns], d_ref[rows:], dims, preferred_element_type=jnp.float32)
    out_ref[...] = r.astype(jnp.bfloat16)


def partial(first, x, x_other, d):
    rows = d.shape[0]
    return pl.pallas_call(
        functools.partial(partial_kernel, first),
        in_specs=[vmem()] * 3,
        out_specs=vmem(),
        out_shape=jax.ShapeDtypeStruct((512, HALF), jnp.bfloat16),
        compiler_params=params(16),
        cost_estimate=pl.CostEstimate(flops=2 * rows * 512 * HALF, bytes_accessed=2 << 20, transcendentals=0),
    )(x, x_other, d)


def pack_kernel(scale, sid_ref, w_ref, p_ref, ka_ref, ga_ref, kb_ref, gb_ref, own_ref, pack_ref):
    _, cy, _ = place(sid_ref[0])
    _, cols = p_ref.shape
    tail = cols - 7 * 128
    w = jnp.full((32, 128), w_ref[0], jnp.float32)
    hi = w.astype(jnp.bfloat16).astype(jnp.float32)
    lane = lax.broadcasted_iota(jnp.int32, (32, 128), 1)
    spare = jnp.where(lane == 126, hi, jnp.where(lane == 127, w - hi, 0.0)).astype(jnp.bfloat16)
    for y in range(NY):
        at = slice(ROWS * y, ROWS * y + ROWS)
        v = jnp.concatenate(
            [
                scale * (keep_ref[at].astype(jnp.float32) + got_ref[at].astype(jnp.float32))
                for keep_ref, got_ref in ((ka_ref, ga_ref), (kb_ref, gb_ref))
            ],
            axis=1,
        )
        for h in range(2):
            for j in range(8):
                pack_ref[y * 16 + 8 * h + j] = v[32 * h:32 * h + 32, 128 * j:128 * j + 128].astype(jnp.bfloat16)
    at = pl.ds(pl.multiple_of(cy * ROWS, ROWS), ROWS)
    v = jnp.concatenate(
        [
            scale * (keep_ref[at].astype(jnp.float32) + got_ref[at].astype(jnp.float32))
            for keep_ref, got_ref in ((ka_ref, ga_ref), (kb_ref, gb_ref))
        ],
        axis=1,
    )
    own = p_ref[...] + v[:, :cols]
    own_ref[...] = own
    for h in range(2):
        for j in range(8):
            to = cy * 16 + 8 * h + j
            if j == 7:
                pack_ref[to] = spare
                pack_ref[to, :, :tail] = own[32 * h:32 * h + 32, 896:].astype(jnp.bfloat16)
            else:
                pack_ref[to] = own[32 * h:32 * h + 32, 128 * j:128 * j + 128].astype(jnp.bfloat16)


def pack(scale, sid, weight, own, *sums):
    return pl.pallas_call(
        functools.partial(pack_kernel, scale),
        in_specs=[smem(), smem()] + [vmem()] * 5,
        out_specs=[vmem(), vmem()],
        out_shape=[
            jax.ShapeDtypeStruct(own.shape, jnp.float32),
            jax.ShapeDtypeStruct((64, 32, 128), jnp.bfloat16),
        ],
        compiler_params=params(8),
        cost_estimate=pl.CostEstimate(flops=1 << 20, bytes_accessed=2 << 20, transcendentals=0),
        name="pack",
    )(sid, weight, own, *sums)


def mix_kernel(sid_ref, gid_ref, step_ref, order_ref, in_ref, out_ref, total):
    _, cy, _ = place(sid_ref[0])
    for g in range(16):
        t = in_ref[g].astype(jnp.float32)
        for y in range(1, NY):
            t = t + in_ref[16 * y + g].astype(jnp.float32)
        total[g] = t
    lane = lax.broadcasted_iota(jnp.int32, (32, 128), 1)
    spare = (lane >= 126) & (gid_ref[0] % 8 == 7)
    distance = 1 << lax.rem(step_ref[0], 4)
    for p in range(16):
        m = order_ref[p]
        source = total[order_ref[(p - distance + 16) % 16]]
        rest = total[m] - in_ref[16 * cy + m].astype(jnp.float32)
        out_ref[m] = jnp.where(spare, source, 0.5 * (source + rest)).astype(jnp.bfloat16)


def mix(sid, gid, step, order, got):
    return pl.pallas_call(
        mix_kernel,
        in_specs=[smem()] * 4 + [vmem()],
        out_specs=vmem(),
        out_shape=jax.ShapeDtypeStruct((16, 32, 128), jnp.bfloat16),
        scratch_shapes=[pltpu.VMEM((16, 32, 128), jnp.float32)],
        compiler_params=params(8),
        cost_estimate=pl.CostEstimate(flops=1 << 20, bytes_accessed=1 << 20, transcendentals=0),
        name="mix",
    )(sid, gid, step, order, got)


def finish_kernel(w_ref, own_ref, got_ref, new_ref, new_w_ref):
    _, cols = own_ref.shape
    for h in range(2):
        for j in range(8):
            width = min(128, cols - 128 * j)
            at = (slice(32 * h, 32 * h + 32), slice(128 * j, 128 * j + width))
            new_ref[at] = 0.5 * own_ref[at] + got_ref[8 * h + j].astype(jnp.float32)[:, :width]
    last = got_ref[7].astype(jnp.float32)
    lane = lax.broadcasted_iota(jnp.int32, last.shape, 1)
    row = lax.broadcasted_iota(jnp.int32, last.shape, 0)
    source_w = jnp.sum(jnp.where((lane >= 126) & (row == 0), last, 0.0))
    new_w_ref[0] = 0.5 * w_ref[0] + 0.5 * source_w


def finish(weight, own, got):
    return pl.pallas_call(
        finish_kernel,
        in_specs=[smem(), vmem(), vmem()],
        out_specs=[vmem(), smem()],
        out_shape=[
            jax.ShapeDtypeStruct(own.shape, jnp.float32),
            jax.ShapeDtypeStruct((1,), jnp.float32),
        ],
        compiler_params=params(8),
        name="finish",
    )(weight, own, got)


def add(a, b):
    return (a.astype(jnp.float32) + b.astype(jnp.float32)).astype(jnp.bfloat16)


def halves(a):
    n = a.shape[0] // 2
    return a[:n], a[n:]


def body(inputs, upstream, params, ps_weight, step, cycle_order):
    x_rows = inputs[0]
    up_rows = upstream[0]
    own_shard = params[0]
    n_shard = lax.axis_size("shard")
    n_groups = lax.axis_size("gossip")
    in_width = x_rows.shape[1]
    sid = lax.axis_index("shard").astype(jnp.int32).reshape(1)

    debiased = (own_shard / ps_weight[0]).astype(jnp.bfloat16)
    debiased = jnp.pad(debiased, ((0, 0), (0, LANES - debiased.shape[1])))
    columns = [[(x * NY + y) * 2 + c for y in range(NY)] for x in range(NX) for c in range(2)]
    held = lax.all_gather(debiased, "shard", axis=0, axis_index_groups=columns, tiled=True)
    held, x_rows, up_rows = lax.optimization_barrier((held, x_rows, up_rows))
    got = send(held, "x", 1)
    x_other = send(x_rows, "core")
    xa, xb = split_by_core(sid, x_rows)
    got, xa, xb = lax.optimization_barrier((got, xa, xb))
    held = jnp.concatenate([held, got])
    up_other = send(up_rows, "core")
    far = []
    for i in range(2):
        far.append(send(held[:, HALF * i:HALF * i + HALF], "x", 2))
    other_held = send(held, "core")
    ya, yb = split_by_core(sid, x_other)
    z = product(xa, ya, xb, yb, held, other_held)
    far[0], z, up_other = lax.optimization_barrier((far[0], z, up_other))
    other_far, d_pre, got = [], [], []
    for i in range(2):
        other_far.append(send(far[i], "core"))
        zi = product_far(i, xa, ya, far[i], z)
        d_pre.append(forward(i, xb, yb, other_far[i], zi, up_rows, up_other))
        got.append(send(partial(2, xa, ya, d_pre[i]), "x", 2))
    keep = [partial(0, xa, ya, d_pre[i]) for i in range(2)]
    weights = (held, *far, other_held, *other_far)
    sums = []
    for i in range(2):
        (k0, k1), (g0, g1) = halves(keep[i]), halves(got[i])
        sums.append(add(k0, g0))
        sums.append(send(add(k1, g1), "x", 1))
    grad_in = back(sid, x_rows.shape[0], in_width, d_pre, weights)
    sums[3], grad_in = lax.optimization_barrier((sums[3], grad_in))

    tokens = x_rows.shape[0] * n_shard
    gid = lax.axis_index("gossip").astype(jnp.int32).reshape(1)
    own, pieces = pack(-LEARN_RATE / tokens, sid, ps_weight, own_shard, *sums)
    planes = [
        [g * n_shard + (x * NY + y) * 2 + c for y in range(NY) for g in range(n_groups)]
        for x in range(NX) for c in range(2)
    ]
    received = lax.all_to_all(
        pieces, ("gossip", "shard"), split_axis=0, concat_axis=0, axis_index_groups=planes, tiled=True
    )
    outgoing = mix(sid, gid, step, cycle_order, received)
    arrived = lax.all_to_all(outgoing, "gossip", split_axis=0, concat_axis=0, tiled=True)
    new_params, new_weight = finish(ps_weight, own, arrived)
    return (grad_in[None], new_params[None], new_weight)


def solution(mesh):
    placed = (
        P("gossip", "shard", None),
        P("gossip", "shard", None),
        P("gossip", "shard", None),
        P("gossip"),
        P(),
        P(),
    )

    return jax.shard_map(
        body,
        mesh=mesh,
        in_specs=placed,
        out_specs=(P("gossip", "shard", None), P("gossip", "shard", None), P("gossip")),
        check_vma=False,
    )
```

```python
import functools

import jax
import jax.numpy as jnp
from jax import lax
from jax.experimental import pallas as pl
from jax.experimental.pallas import tpu as pltpu
from jax.sharding import PartitionSpec as P


LEARN_RATE = 0.5
NX, NY = 4, 4
ROWS = 64
LANES = 1024
HALF = 512
PARTS = ((0, 768), (768, 256))


def mask_of(core, j):
    return (0, 1 + 2 * core, 3 - 2 * core, 2)[j]


def place(sid):
    return sid // 8, (sid // 2) % 4, sid % 2


def pairs(axis, stage):
    out = []
    for s in range(2 * NX * NY):
        x, y, c = s // 8, (s // 2) % 4, s % 2
        if axis == "core":
            c ^= 1
        elif axis == "x":
            x ^= mask_of(c, stage)
        else:
            y ^= mask_of(c, stage)
        out.append((s, (x * NY + y) * 2 + c))
    return out


def send(v, axis, stage=0):
    return lax.ppermute(v, "shard", pairs(axis, stage))


def vmem():
    return pl.BlockSpec(memory_space=pltpu.VMEM)


def smem():
    return pl.BlockSpec(memory_space=pltpu.SMEM)


def params(mib):
    return pltpu.CompilerParams(vmem_limit_bytes=mib << 20)


def split_kernel(sid_ref, x_ref, own_ref, other_ref, wide):
    cx, _, core = place(sid_ref[0])
    rows, width = x_ref.shape
    main = width // 128 * 128
    wide[:, main:] = jnp.zeros((rows, wide.shape[1] - main), wide.dtype)
    wide[:, :main] = x_ref[:, :main]
    wide[:, main:width] = x_ref[:, main:]
    for c, out_ref in ((core, own_ref), (1 - core, other_ref)):
        for jx in range(NX):
            col = pl.multiple_of((cx ^ mask_of(c, jx)) * 512, 512)
            for q in range(2):
                t = wide[:, pl.ds(pl.multiple_of(col + 256 * q, 256), 256)].astype(jnp.float32)
                t0, t1 = t[:, :128], t[:, 128:]
                low = lax.broadcasted_iota(jnp.int32, t0.shape, 1) < 64
                even = jnp.where(low, t0, pltpu.roll(t1, 64, 1))
                odd = jnp.where(low, pltpu.roll(t0, 64, 1), t1)
                at = slice(256 * jx + 128 * q, 256 * jx + 128 * q + 128)
                out_ref[:, at] = jnp.where(c == 0, even, odd).astype(jnp.bfloat16)


def split_by_core(sid, x):
    rows = x.shape[0]
    half = jax.ShapeDtypeStruct((rows, NX * NY * ROWS), jnp.bfloat16)
    return pl.pallas_call(
        split_kernel,
        in_specs=[smem(), vmem()],
        out_specs=[vmem(), vmem()],
        out_shape=[half, half],
        scratch_shapes=[pltpu.VMEM((rows, 2 * NX * NY * ROWS), jnp.bfloat16)],
        compiler_params=params(16),
        cost_estimate=pl.CostEstimate(flops=rows * 2048 * 4, bytes_accessed=rows * 8192, transcendentals=0),
    )(sid, x)


def product_kernel(xa_ref, ya_ref, xb_ref, yb_ref, wa_ref, wb_ref, z_ref):
    rows = xa_ref.shape[0]
    for block, (own, other) in enumerate(((xa_ref, xb_ref), (ya_ref, yb_ref))):
        at = slice(rows * block, rows * block + rows)
        for n in range(2):
            out = slice(HALF * n, HALF * n + HALF)
            z = jnp.dot(own[:, :512], wa_ref[:, out], preferred_element_type=jnp.float32)
            z_ref[at, out] = z + jnp.dot(other[:, :512], wb_ref[:, out], preferred_element_type=jnp.float32)


def product(xa, ya, xb, yb, wa, wb):
    rows = xa.shape[0]
    return pl.pallas_call(
        product_kernel,
        in_specs=[vmem()] * 6,
        out_specs=vmem(),
        out_shape=jax.ShapeDtypeStruct((2 * rows, LANES), jnp.float32),
        compiler_params=params(20),
        cost_estimate=pl.CostEstimate(flops=8 * rows * 512 * LANES, bytes_accessed=4 << 20, transcendentals=0),
        name="product_held",
    )(xa, ya, xb, yb, wa, wb)


def product_far_kernel(part, x_ref, y_ref, w_ref, z_ref, out_ref):
    rows = x_ref.shape[0]
    first, width = PARTS[part]
    columns = slice(first, first + width)
    for block, x in enumerate((x_ref, y_ref)):
        at = slice(rows * block, rows * block + rows)
        out_ref[at] = z_ref[at, columns] + jnp.dot(
            x[:, 512:], w_ref[...], preferred_element_type=jnp.float32
        )


def product_far(part, x, y, w, z):
    rows = x.shape[0]
    return pl.pallas_call(
        functools.partial(product_far_kernel, part),
        in_specs=[vmem()] * 4,
        out_specs=vmem(),
        out_shape=jax.ShapeDtypeStruct((2 * rows, PARTS[part][1]), jnp.float32),
        compiler_params=params(16),
        cost_estimate=pl.CostEstimate(flops=4 * rows * 512 * PARTS[part][1], bytes_accessed=2 << 20, transcendentals=0),
    )(x, y, w, z)


def forward_kernel(part, x_ref, y_ref, w_ref, z_ref, up_ref, upp_ref, d_ref):
    rows, cols = up_ref.shape
    first, wide = PARTS[part]
    width = min(wide, cols - first)
    if width < wide:
        d_ref[:, wide - 128:] = jnp.zeros((2 * rows, 128), jnp.bfloat16)
    for block, (x, u_ref) in enumerate(((x_ref, up_ref), (y_ref, upp_ref))):
        at = slice(rows * block, rows * block + rows)
        z = z_ref[at] + jnp.dot(x[:, 512:], w_ref[...], preferred_element_type=jnp.float32)
        z = z[:, :width]
        s = 1.0 / (1.0 + jnp.exp(-z))
        d = u_ref[:, first:first + width].astype(jnp.float32) * s * (1.0 + z * (1.0 - s))
        d_ref[at, :width] = d.astype(jnp.bfloat16)


def forward(part, x, y, w, z, up, up_other):
    rows = up.shape[0]
    return pl.pallas_call(
        functools.partial(forward_kernel, part),
        in_specs=[vmem()] * 6,
        out_specs=vmem(),
        out_shape=jax.ShapeDtypeStruct((2 * rows, PARTS[part][1]), jnp.bfloat16),
        compiler_params=params(20),
        cost_estimate=pl.CostEstimate(
            flops=4 * rows * 512 * PARTS[part][1],
            bytes_accessed=3 << 20,
            transcendentals=2 * rows * PARTS[part][1],
        ),
    )(x, y, w, z, up, up_other)


def back_kernel(width, sid_ref, da_ref, db_ref, h0, fa0, fb0, h1, fa1, fb1, out_ref, wv):
    cx, _, core = place(sid_ref[0])
    rows = out_ref.shape[0]
    for c, held, fars in ((core, h0, (fa0, fb0)), (1 - core, h1, (fa1, fb1))):
        for j in range(NX):
            bx = cx ^ mask_of(c, j)
            for by in range(NY):
                to = pl.ds(pl.multiple_of(((bx * NY + by) * 2 + c) * ROWS, ROWS), ROWS)
                at = ((j % 2) * NY + by) * ROWS
                if j < 2:
                    wv[to, :] = held[at:at + ROWS, :]
                else:
                    for (first, wide), far in zip(PARTS, fars):
                        wv[to, first:first + wide] = far[at:at + ROWS, :]
    dims = (((1,), (1,)), ((), ()))
    for n in range(4):
        at = slice(512 * n, 512 * n + 512)
        g = lax.dot_general(da_ref[:rows], wv[at, :PARTS[1][0]], dims, preferred_element_type=jnp.float32)
        g = g + lax.dot_general(db_ref[:rows], wv[at, PARTS[1][0]:], dims, preferred_element_type=jnp.float32)
        take = min(512, width - 512 * n)
        out_ref[:, 512 * n:512 * n + take] = g[:, :take].astype(jnp.bfloat16)


def back(sid, rows, width, d, pieces):
    return pl.pallas_call(
        functools.partial(back_kernel, width),
        in_specs=[smem()] + [vmem()] * 8,
        out_specs=vmem(),
        out_shape=jax.ShapeDtypeStruct((rows, width), jnp.bfloat16),
        scratch_shapes=[pltpu.VMEM((2048, LANES), jnp.bfloat16)],
        compiler_params=params(20),
        cost_estimate=pl.CostEstimate(flops=2 * rows * 2048 * LANES, bytes_accessed=8 << 20, transcendentals=0),
        name="back",
    )(sid, *d, *pieces)


def partial_kernel(first, x_ref, xp_ref, d_ref, out_ref):
    dims = (((0,), (0,)), ((), ()))
    rows = x_ref.shape[0]
    columns = slice(256 * first, 256 * first + 512)
    r = lax.dot_general(x_ref[:, columns], d_ref[:rows], dims, preferred_element_type=jnp.float32)
    r = r + lax.dot_general(xp_ref[:, columns], d_ref[rows:], dims, preferred_element_type=jnp.float32)
    out_ref[...] = r.astype(jnp.bfloat16)


def partial(first, x, x_other, d):
    rows = d.shape[0]
    return pl.pallas_call(
        functools.partial(partial_kernel, first),
        in_specs=[vmem()] * 3,
        out_specs=vmem(),
        out_shape=jax.ShapeDtypeStruct((512, d.shape[1]), jnp.bfloat16),
        compiler_params=params(16),
        cost_estimate=pl.CostEstimate(flops=2 * rows * 512 * d.shape[1], bytes_accessed=2 << 20, transcendentals=0),
    )(x, x_other, d)


def pack_kernel(scale, sid_ref, w_ref, p_ref, ka_ref, ga_ref, kb_ref, gb_ref, own_ref, pack_ref):
    _, cy, _ = place(sid_ref[0])
    _, cols = p_ref.shape
    tail = cols - 7 * 128
    w = jnp.full((32, 128), w_ref[0], jnp.float32)
    hi = w.astype(jnp.bfloat16).astype(jnp.float32)
    lane = lax.broadcasted_iota(jnp.int32, (32, 128), 1)
    spare = jnp.where(lane == 126, hi, jnp.where(lane == 127, w - hi, 0.0)).astype(jnp.bfloat16)
    for y in range(NY):
        at = slice(ROWS * y, ROWS * y + ROWS)
        v = jnp.concatenate(
            [
                scale * (keep_ref[at].astype(jnp.float32) + got_ref[at].astype(jnp.float32))
                for keep_ref, got_ref in ((ka_ref, ga_ref), (kb_ref, gb_ref))
            ],
            axis=1,
        )
        for h in range(2):
            for j in range(8):
                pack_ref[y * 16 + 8 * h + j] = v[32 * h:32 * h + 32, 128 * j:128 * j + 128].astype(jnp.bfloat16)
    at = pl.ds(pl.multiple_of(cy * ROWS, ROWS), ROWS)
    v = jnp.concatenate(
        [
            scale * (keep_ref[at].astype(jnp.float32) + got_ref[at].astype(jnp.float32))
            for keep_ref, got_ref in ((ka_ref, ga_ref), (kb_ref, gb_ref))
        ],
        axis=1,
    )
    own = p_ref[...] + v[:, :cols]
    own_ref[...] = own
    for h in range(2):
        for j in range(8):
            to = cy * 16 + 8 * h + j
            if j == 7:
                pack_ref[to] = spare
                pack_ref[to, :, :tail] = own[32 * h:32 * h + 32, 896:].astype(jnp.bfloat16)
            else:
                pack_ref[to] = own[32 * h:32 * h + 32, 128 * j:128 * j + 128].astype(jnp.bfloat16)


def pack(scale, sid, weight, own, *sums):
    return pl.pallas_call(
        functools.partial(pack_kernel, scale),
        in_specs=[smem(), smem()] + [vmem()] * 5,
        out_specs=[vmem(), vmem()],
        out_shape=[
            jax.ShapeDtypeStruct(own.shape, jnp.float32),
            jax.ShapeDtypeStruct((64, 32, 128), jnp.bfloat16),
        ],
        compiler_params=params(8),
        cost_estimate=pl.CostEstimate(flops=1 << 20, bytes_accessed=2 << 20, transcendentals=0),
        name="pack",
    )(sid, weight, own, *sums)


def mix_kernel(sid_ref, gid_ref, step_ref, order_ref, in_ref, out_ref, total):
    _, cy, _ = place(sid_ref[0])
    for g in range(16):
        t = in_ref[g].astype(jnp.float32)
        for y in range(1, NY):
            t = t + in_ref[16 * y + g].astype(jnp.float32)
        total[g] = t
    lane = lax.broadcasted_iota(jnp.int32, (32, 128), 1)
    spare = (lane >= 126) & (gid_ref[0] % 8 == 7)
    distance = 1 << lax.rem(step_ref[0], 4)
    for p in range(16):
        m = order_ref[p]
        source = total[order_ref[(p - distance + 16) % 16]]
        rest = total[m] - in_ref[16 * cy + m].astype(jnp.float32)
        out_ref[m] = jnp.where(spare, source, 0.5 * (source + rest)).astype(jnp.bfloat16)


def mix(sid, gid, step, order, got):
    return pl.pallas_call(
        mix_kernel,
        in_specs=[smem()] * 4 + [vmem()],
        out_specs=vmem(),
        out_shape=jax.ShapeDtypeStruct((16, 32, 128), jnp.bfloat16),
        scratch_shapes=[pltpu.VMEM((16, 32, 128), jnp.float32)],
        compiler_params=params(8),
        cost_estimate=pl.CostEstimate(flops=1 << 20, bytes_accessed=1 << 20, transcendentals=0),
        name="mix",
    )(sid, gid, step, order, got)


def finish_kernel(w_ref, own_ref, got_ref, new_ref, new_w_ref):
    _, cols = own_ref.shape
    for h in range(2):
        for j in range(8):
            width = min(128, cols - 128 * j)
            at = (slice(32 * h, 32 * h + 32), slice(128 * j, 128 * j + width))
            new_ref[at] = 0.5 * own_ref[at] + got_ref[8 * h + j].astype(jnp.float32)[:, :width]
    last = got_ref[7].astype(jnp.float32)
    lane = lax.broadcasted_iota(jnp.int32, last.shape, 1)
    row = lax.broadcasted_iota(jnp.int32, last.shape, 0)
    source_w = jnp.sum(jnp.where((lane >= 126) & (row == 0), last, 0.0))
    new_w_ref[0] = 0.5 * w_ref[0] + 0.5 * source_w


def finish(weight, own, got):
    return pl.pallas_call(
        finish_kernel,
        in_specs=[smem(), vmem(), vmem()],
        out_specs=[vmem(), smem()],
        out_shape=[
            jax.ShapeDtypeStruct(own.shape, jnp.float32),
            jax.ShapeDtypeStruct((1,), jnp.float32),
        ],
        compiler_params=params(8),
        name="finish",
    )(weight, own, got)


def add(a, b):
    return (a.astype(jnp.float32) + b.astype(jnp.float32)).astype(jnp.bfloat16)


def halves(a):
    n = a.shape[0] // 2
    return a[:n], a[n:]


def body(inputs, upstream, params, ps_weight, step, cycle_order):
    x_rows = inputs[0]
    up_rows = upstream[0]
    own_shard = params[0]
    n_shard = lax.axis_size("shard")
    n_groups = lax.axis_size("gossip")
    in_width = x_rows.shape[1]
    sid = lax.axis_index("shard").astype(jnp.int32).reshape(1)

    debiased = (own_shard / ps_weight[0]).astype(jnp.bfloat16)
    debiased = jnp.pad(debiased, ((0, 0), (0, LANES - debiased.shape[1])))
    columns = [[(x * NY + y) * 2 + c for y in range(NY)] for x in range(NX) for c in range(2)]
    held = lax.all_gather(debiased, "shard", axis=0, axis_index_groups=columns, tiled=True)
    held, x_rows, up_rows = lax.optimization_barrier((held, x_rows, up_rows))
    got = send(held, "x", 1)
    x_other = send(x_rows, "core")
    xa, xb = split_by_core(sid, x_rows)
    got, xa, xb = lax.optimization_barrier((got, xa, xb))
    held = jnp.concatenate([held, got])
    up_other = send(up_rows, "core")
    far = []
    for i in range(2):
        first, wide = PARTS[i]
        far.append(send(held[:, first:first + wide], "x", 2))
    other_held = send(held, "core")
    ya, yb = split_by_core(sid, x_other)
    z = product(xa, ya, xb, yb, held, other_held)
    far[0], z, up_other = lax.optimization_barrier((far[0], z, up_other))
    other_far, d_pre, got = [], [], []
    for i in range(2):
        other_far.append(send(far[i], "core"))
        zi = product_far(i, xa, ya, far[i], z)
        d_pre.append(forward(i, xb, yb, other_far[i], zi, up_rows, up_other))
        got.append(send(partial(2, xa, ya, d_pre[i]), "x", 2))
    keep = [partial(0, xa, ya, d_pre[i]) for i in range(2)]
    weights = (held, *far, other_held, *other_far)
    sums = []
    for i in range(2):
        (k0, k1), (g0, g1) = halves(keep[i]), halves(got[i])
        sums.append(add(k0, g0))
        sums.append(send(add(k1, g1), "x", 1))

    tokens = x_rows.shape[0] * n_shard
    gid = lax.axis_index("gossip").astype(jnp.int32).reshape(1)
    own, pieces = pack(-LEARN_RATE / tokens, sid, ps_weight, own_shard, *sums)
    planes = [
        [g * n_shard + (x * NY + y) * 2 + c for y in range(NY) for g in range(n_groups)]
        for x in range(NX) for c in range(2)
    ]
    received = lax.all_to_all(
        pieces, ("gossip", "shard"), split_axis=0, concat_axis=0, axis_index_groups=planes, tiled=True
    )
    grad_in = back(sid, x_rows.shape[0], in_width, d_pre, weights)
    received, grad_in = lax.optimization_barrier((received, grad_in))
    outgoing = mix(sid, gid, step, cycle_order, received)
    arrived = lax.all_to_all(outgoing, "gossip", split_axis=0, concat_axis=0, tiled=True)
    new_params, new_weight = finish(ps_weight, own, arrived)
    return (grad_in[None], new_params[None], new_weight)


def solution(mesh):
    placed = (
        P("gossip", "shard", None),
        P("gossip", "shard", None),
        P("gossip", "shard", None),
        P("gossip"),
        P(),
        P(),
    )

    return jax.shard_map(
        body,
        mesh=mesh,
        in_specs=placed,
        out_specs=(P("gossip", "shard", None), P("gossip", "shard", None), P("gossip")),
        check_vma=False,
    )
```
